32 devices in a mesh: dp: 8 (over z, y), table: 4 (over x, core).
Axes of the slice: x: 2, y: 2, z: 4, core: 2. Of those that a mesh axis runs over, the one named last changes fastest.
Arguments:
- expr: bfloat16 [64, 128, 768], P(('dp', 'table')), may hold values from -6 to 6
- gene_owner: int32 [64, 128, 1], P(('dp', 'table')), may hold values from 0 to 7; in each aligned block of 1024 rows (0 to 1023, 1024 to 2047, ..., all dimensions but the last counted through in order) at most 192 rows name the same one
- gene_row: int32 [64, 128], P(('dp', 'table')), may hold values from 0 to 4607
- lengths: int32 [64], P(('dp', 'table')), may hold values from 1 to 128, 6144 in all
- cotangent: bfloat16 [64, 128, 768], P(('dp', 'table')), may hold values from -6 to 6
- tables: bfloat16 [4, 36864, 768], P('table', 'dp'), may hold values from -3 to 3
- w_qkv: bfloat16 [768, 2304], P(('dp', 'table')), may hold values from -0.21875 to 0.21875
- w_out: bfloat16 [768, 768], P(('dp', 'table')), may hold values from -0.875 to 0.875
- w_up: bfloat16 [768, 3072], P(('dp', 'table')), may hold values from -0.21875 to 0.21875
- w_down: bfloat16 [3072, 768], P(('dp', 'table')), may hold values from -0.109375 to 0.109375
- gains: bfloat16 [2, 768], P(None, ('dp', 'table')), may hold values from 0.5 to 1.5
- biases: bfloat16 [6, 768], P(None, ('dp', 'table')), may hold values from -2 to 2
- up_bias: bfloat16 [3072], P(('dp', 'table')), may hold values from -2 to 2
Outputs:
- out: bfloat16 [64, 128, 768], P(('dp', 'table'))
- grad_expr: float32 [64, 128, 768], P(('dp', 'table'))
- grad_tables: float32 [4, 36864, 768], P('table', 'dp')
- grad_w_qkv: float32 [768, 2304], P(('dp', 'table'))
- grad_w_out: float32 [768, 768], P(('dp', 'table'))
- grad_w_up: float32 [768, 3072], P(('dp', 'table'))
- grad_w_down: float32 [3072, 768], P(('dp', 'table'))
- grad_gains: float32 [2, 768], P(None, ('dp', 'table'))
- grad_biases: float32 [6, 768], P(None, ('dp', 'table'))
- grad_up_bias: float32 [3072], P(('dp', 'table'))
The draws below stay inside these ranges and needn't reach their ends.
Inputs may be any that keep to these rules, and one draw needn't show every extreme that they name: `gene_owner`: in each aligned block of 1024 positions (the slots of the devices that share a dp index), no owner is named more than 192 times, a bound that some block reaches. `lengths`: some slot has length 128.
All inputs are finite; a program needn't handle non-finite values. No bound on the sum of `lengths` on one device may be relied on, other than what follows from the above.
Results may differ from the reference program's by a relative error of at most 0.039.
Values may be sent and summed in bfloat16 or wider, within the bound.
A program may use at most 192 MiB of HBM per device.

```python
import math
import jax
import jax.numpy as jnp
import numpy as np
from jax import lax

D = 768
HEADS = 12
HEAD_DIM = 64
FF = 3072
SEQ = 128
ROWS = 36864
TABLES = 4
ROWS_DEV = 4608
TOK_DEV = 256
SLOTS = 64
CAP = 192
N_DP = 8


def touch_ends(values, rng, smallest, high):
    dims = values.shape
    place = [jax.random.randint(jax.random.fold_in(rng, axis), (), 0, dims[axis]) for axis in range(len(dims))]
    values = values.at[tuple(place)].set(smallest)
    longest = dims.index(max(dims))
    place[longest] = (place[longest] + 1) % dims[longest]
    return values.at[tuple(place)].set(high)


def level_of(rng, dims, shards, least, largest):
    gain = 1.0
    for position, blocks in shards:
        draws = jax.random.uniform(jax.random.fold_in(jax.random.fold_in(rng, 6), position), (blocks,), jnp.float32, least / len(shards), largest / len(shards))
        gain = gain * jnp.repeat(jnp.exp(draws), dims[position] // blocks).reshape((-1,) + (1,) * (len(dims) - 1 - position))
    return gain


def split_up(count, total, limit, skew):
    weights = [(1 << 20) // math.isqrt(grade ** skew) + 1 for grade in range(2, count + 1)]
    surplus, given = total - limit - (count - 1), [1] * (count - 1)
    while surplus > 0:
        candidates = [i for i in range(count - 1) if given[i] < limit]
        mass, remaining = sum([weights[i] for i in candidates]), surplus
        for i in candidates:
            addition = min(limit - given[i], max(1, remaining * weights[i] // mass), surplus)
            given[i] = given[i] + addition
            surplus = surplus - addition
    return np.array([limit] + given)


def uneven_parts(own_key, number_of, total, most, lean):
    if number_of == 2:
        one = jax.random.randint(own_key, (), max(1, total - most), min(most, total - 1) + 1)
        return jnp.stack([one, total - one])
    tallies = jnp.asarray(split_up(number_of, total, most, lean), jnp.int32)
    couples = (number_of - 1) // 2
    source_of, sink = tallies[1:1 + 2 * couples:2], tallies[2:2 + 2 * couples:2]
    margin = jnp.minimum(source_of - 1, most - sink)
    shifted = jax.random.randint(jax.random.fold_in(own_key, 1), (couples,), 0, 1 << 20) % (margin + 1)
    tallies = tallies.at[1:1 + 2 * couples:2].set(source_of - shifted).at[2:2 + 2 * couples:2].set(sink + shifted)
    return tallies[jax.random.permutation(jax.random.fold_in(own_key, 2), number_of)]


def shared_out(stream_key, own, number, rows, amount, top, reach, skew):
    order = jax.random.permutation(stream_key, amount)
    heavy_load, ordinary = load_shares(amount, rows * top, reach, skew, True), load_shares(amount, rows * top, reach, skew, False)
    places = jnp.arange(amount)

    def named(sizes, offset_by):
        used = int((sizes > 0).sum())
        fixed = max(1, used // 4)
        moved = fixed + (places - fixed + offset_by * (used - fixed)) % max(1, amount - fixed)
        return jnp.zeros((amount,), jnp.int32).at[order[jnp.where(places < fixed, places, moved)]].set(jnp.asarray(sizes, jnp.int32))

    sizes = jnp.where(number % 4 == 0, named(heavy_load, number // 4), named(ordinary, number - number // 4 - 1))
    mixed = jax.random.permutation(jax.random.fold_in(own, 3), amount)
    donor, receiver = mixed[0:amount // 2 * 2:2], mixed[1:amount // 2 * 2:2]
    slack = jnp.minimum(sizes[donor] - 1, reach - sizes[receiver]) // 2
    slack = jnp.where((donor == order[0]) | (receiver == order[0]) | (sizes[receiver] == 0), 0, jnp.maximum(slack, 0))
    moved = jax.random.randint(jax.random.fold_in(own, 4), (amount // 2,), 0, 1 << 20) % (slack + 1)
    sizes = sizes.at[donor].add(-moved).at[receiver].add(moved)
    members = jnp.searchsorted(jnp.cumsum(sizes), jnp.arange(rows * top), side="right").astype(jnp.int32)
    table = members.reshape(top, rows).T
    table = table[jax.random.permutation(jax.random.fold_in(own, 1), rows)]
    offset_by = jax.random.randint(jax.random.fold_in(own, 2), (rows, 1), 0, top)
    return jnp.take_along_axis(table, (jnp.arange(top)[None, :] + offset_by) % top, axis=1)


def load_shares(count, total, limit, skew, full):
    loads = [(1 << 20) // math.isqrt(grade ** skew) + 1 for grade in range(1, count + 1)]
    largest = limit if full else min(limit, max(-(-total // count), total * loads[0] // sum(loads)))
    least = 1 if total - largest >= count - 1 else 0
    given, spare = [largest] + [least] * (count - 1), total - largest - least * (count - 1)
    while spare > 0:
        movable = [i for i in range(1, count) if given[i] < largest] or [i for i in range(1, count) if given[i] < limit]
        pool, remaining = sum([loads[i] for i in movable]), spare
        for i in movable:
            addition = min(limit - given[i], max(1, remaining * loads[i] // pool), spare)
            given[i] = given[i] + addition
            spare = spare - addition
    return np.array(given)


def normal_values(own_key, extent, width, most, pieces=(), held_as=jnp.bfloat16):
    level = level_of(own_key, extent, pieces, -0.22, 0.18) if pieces else 1.0
    array = jax.random.normal(own_key, extent, jnp.float32) * width * level
    return jnp.minimum(jnp.maximum(array, -most), most).astype(held_as)


def setup_inputs(seed: int = 0) -> dict:
    keys = jax.random.split(jax.random.key(seed), 14)
    expr = normal_values(keys[0], (SLOTS, SEQ, D), 1.0, 6.0, ((0, 32),))
    gene_owner_keys = jax.random.split(jax.random.fold_in(keys[1], 1), SLOTS * SEQ // (TABLES * TOK_DEV))
    gene_owner_turns = jax.random.permutation(jax.random.fold_in(keys[1], 3), SLOTS * SEQ // (TABLES * TOK_DEV))
    gene_owner = jax.vmap(lambda own, number: shared_out(jax.random.fold_in(keys[1], 2), own, number, TABLES * TOK_DEV, N_DP, 1, CAP, 1))(gene_owner_keys, gene_owner_turns).reshape((SLOTS, SEQ, 1))
    gene_row = touch_ends(jax.random.randint(keys[2], (SLOTS, SEQ), 0, ROWS_DEV), jax.random.fold_in(keys[2], 1), 0, ROWS_DEV - 1).astype(jnp.int32)
    lengths = uneven_parts(keys[3], SLOTS, 3 * SLOTS * SEQ // 4, SEQ, 0).astype(jnp.int32)
    cotangent = normal_values(keys[4], (SLOTS, SEQ, D), 1.0, 6.0, ((0, 32),))
    tables = normal_values(keys[5], (TABLES, ROWS, D), 0.5, 3.0, ((0, 4), (1, 8)))
    w_qkv = normal_values(keys[6], (D, 3 * D), D ** -0.5, 0.21875, ((0, 32),))
    w_out = normal_values(keys[7], (D, D), (D // 16) ** -0.5, 0.875, ((0, 32),))
    w_up = normal_values(keys[8], (D, FF), D ** -0.5, 0.21875, ((0, 32),))
    w_down = normal_values(keys[9], (FF, D), FF ** -0.5, 0.109375, ((0, 32),))
    gains = jnp.clip(1.0 + 0.1 * jax.random.normal(keys[10], (2, D), jnp.float32), 0.5, 1.5).astype(jnp.bfloat16)
    biases = normal_values(keys[11], (6, D), 0.3, 2.0, ((1, 32),))
    up_bias = normal_values(keys[12], (FF,), 0.3, 2.0, ((0, 32),))
    return {"expr": expr, "gene_owner": gene_owner, "gene_row": gene_row, "lengths": lengths, "cotangent": cotangent, "tables": tables, "w_qkv": w_qkv, "w_out": w_out, "w_up": w_up, "w_down": w_down, "gains": gains, "biases": biases, "up_bias": up_bias}


@jax.custom_vjp
def low(v):
    return lax.optimization_barrier(v.astype(jnp.bfloat16)).astype(jnp.float32)

@jax.custom_vjp
def low_back(v):
    return v

def low_keep(v):
    return (low(v), None)

def low_pass(kept, grad):
    return (grad,)

def back_keep(v):
    return (v, None)

def back_low(kept, grad):
    return (low(grad),)
low.defvjp(low_keep, low_pass)
low_back.defvjp(back_keep, back_low)

def layer_norm(values, scale, shift):
    center = values - lax.optimization_barrier(jnp.mean(values, axis=-1, keepdims=True))
    spread = lax.optimization_barrier(jnp.mean(center * center, axis=-1, keepdims=True))
    return center * lax.rsqrt(spread + 1e-05) * scale + shift

def gelu_exact(values):
    return jax.nn.gelu(values, approximate=False)

def reference(expr, gene_owner, gene_row, lengths, cotangent, tables, w_qkv, w_out, w_up, w_down, gains, biases, up_bias):
    highest = lax.Precision.HIGHEST
    group = math.gcd(SLOTS, max(1, 4096 // SEQ))
    rounds = SLOTS // group
    gene_ids = (gene_owner[..., 0] * ROWS_DEV + gene_row).astype(jnp.int32)

    def forward(expr_full, table_full, wqkv, wout, wup, wdown, gain_pair, bias_rows, bias_up):
        qkv_shift = jnp.concatenate([bias_rows[0], jnp.zeros_like(bias_rows[0]), bias_rows[1]])

        def one_group(carry, inputs):
            expr_block, id_block, length_block = inputs
            embedded = table_full[0][id_block]
            for which in range(1, TABLES):
                embedded = embedded + table_full[which][id_block]
            hidden_in = expr_block + embedded
            key_mask = jnp.arange(SEQ)[None, :] < length_block[:, None]
            projected = jnp.einsum('gld,de->gle', low(hidden_in), wqkv, precision=highest) + qkv_shift
            projected = low(low_back(projected)).reshape(group, SEQ, 3, HEADS, HEAD_DIM)
            queries = projected[:, :, 0]
            key_rows = projected[:, :, 1]
            value_rows = projected[:, :, 2]
            scores = low_back(jnp.einsum('gqhd,gkhd->ghqk', queries, key_rows, precision=highest) * 0.125)
            scores = jnp.where(key_mask[:, None, None, :], scores, -1e+30)
            probs = low(jax.nn.softmax(scores, axis=-1))
            mixed = jnp.einsum('ghqk,gkhd->gqhd', probs, value_rows, precision=highest).reshape(group, SEQ, D)
            mixed = low(low_back(mixed))
            branch = low_back(jnp.einsum('gld,de->gle', mixed, wout, precision=highest) + bias_rows[2])
            normed = layer_norm(hidden_in + branch, gain_pair[0], bias_rows[4])
            inner = low_back(jnp.einsum('gld,df->glf', low(normed), wup, precision=highest) + bias_up)
            feed = low_back(jnp.einsum('glf,fd->gld', low(gelu_exact(inner)), wdown, precision=highest) + bias_rows[3])
            final = layer_norm(normed + feed, gain_pair[1], bias_rows[5])
            return (carry, final * key_mask[:, :, None].astype(jnp.float32))
        inputs = (expr_full.reshape(rounds, group, SEQ, D), gene_ids.reshape(rounds, group, SEQ), lengths.reshape(rounds, group))
        _, stacked = lax.scan(jax.checkpoint(one_group), jnp.zeros((), jnp.float32), inputs)
        return stacked.reshape(SLOTS, SEQ, D)
    primals = (expr.astype(jnp.float32), tables.astype(jnp.float32), w_qkv.astype(jnp.float32), w_out.astype(jnp.float32), w_up.astype(jnp.float32), w_down.astype(jnp.float32), gains.astype(jnp.float32), biases.astype(jnp.float32), up_bias.astype(jnp.float32))
    result, backward = jax.vjp(forward, *primals)
    grads = backward(cotangent.astype(jnp.float32))
    return (result.astype(jnp.bfloat16), grads[0], grads[1], grads[2], grads[3], grads[4], grads[5], grads[6], grads[7], grads[8])
```

```python
import jax
import jax.numpy as jnp
from jax import lax
from jax.sharding import PartitionSpec as P

HEAD_DIM = 64
AXES = ("dp", "table")


def layer_norm(values, scale, shift):
    center = values - jnp.mean(values, axis=-1, keepdims=True)
    spread = jnp.mean(center * center, axis=-1, keepdims=True)
    return center * lax.rsqrt(spread + 1e-05) * scale + shift


def gelu_exact(values):
    return jax.nn.gelu(values, approximate=False)


class Grid:
    def __init__(self):
        dp, table = lax.axis_size("dp"), lax.axis_size("table")
        self.count = dp * table
        self.high = dp // 2
        self.side = table // 2
        self.bit_core = 1
        self.bit_x = 2
        self.bit_y = table
        self.bit_z = 2 * table
        me_dp, me_table = lax.axis_index("dp"), lax.axis_index("table")
        self.z, self.y = me_dp // 2, me_dp % 2
        self.x, self.core = me_table // 2, me_table % 2

    def swap(self, value, mask):
        pairs = [(index, index ^ mask) for index in range(self.count)]
        return lax.ppermute(value, AXES, pairs)


def ordered(flag, own, other, axis):
    first = flag == 0
    return jnp.stack([jnp.where(first, own, other), jnp.where(first, other, own)], axis=axis)


def pick(values, index, axis):
    return lax.dynamic_index_in_dim(values, index, axis=axis, keepdims=False)


def gather_chunk(grid, shard, x_first):
    rows = [shard] + [grid.swap(shard, grid.bit_z * step) for step in range(1, grid.high)]
    line = jnp.stack(rows)
    place = jnp.arange(grid.high) ^ grid.z
    line = jnp.stack(
        [
            sum_select([(place[spot] == step, rows[step]) for step in range(grid.high)])
            for spot in range(grid.high)
        ]
    )
    first, second = (grid.bit_x, grid.bit_y) if x_first else (grid.bit_y, grid.bit_x)
    one = grid.swap(line, first)
    two = grid.swap(line, second)
    three = grid.swap(one, second)
    if x_first:
        own_y, other_y = ordered(grid.x, line, one, 1), ordered(grid.x, two, three, 1)
        plane = ordered(grid.y, own_y, other_y, 1)
    else:
        own_x, other_x = ordered(grid.y, line, one, 1), ordered(grid.y, two, three, 1)
        plane = ordered(grid.x, own_x, other_x, 2)
    partner = grid.swap(plane, grid.bit_core)
    whole = ordered(grid.core, plane, partner, 3)
    return whole.reshape((grid.count,) + shard.shape)


def sum_select(choices):
    result = choices[-1][1]
    for test, value in choices[:-1]:
        result = jnp.where(test, value, result)
    return result


def scatter_chunk(grid, grads, x_first):
    rows = grads.shape[0] // grid.count
    blocks = grads.reshape((grid.high, 2, grid.side, 2, rows, grads.shape[1]))
    low = jnp.bfloat16

    def halve(value, flag, axis, bit):
        sent = grid.swap(pick(value, 1 - flag, axis).astype(low), bit)
        return pick(value, flag, axis).astype(jnp.float32) + sent.astype(jnp.float32)

    part = halve(blocks, grid.core, 3, grid.bit_core).astype(low)
    if x_first:
        part = halve(part, grid.x, 2, grid.bit_x).astype(low)
        part = halve(part, grid.y, 1, grid.bit_y).astype(low)
    else:
        part = halve(part, grid.y, 1, grid.bit_y).astype(low)
        part = halve(part, grid.x, 1, grid.bit_x).astype(low)
    total = pick(part, grid.z, 0).astype(jnp.float32)
    for step in range(1, grid.high):
        total = total + grid.swap(pick(part, grid.z ^ step, 0), grid.bit_z * step).astype(jnp.float32)
    return total


def attend_scores(queries, key_rows, key_mask):
    scores = (
        jnp.einsum("sqhd,skhd->shqk", queries, key_rows, preferred_element_type=jnp.float32) * 0.125
    )
    return jnp.where(key_mask[:, None, None, :], scores, -1e30)


def layer_pass(weights, hidden_part, cot_part, length_part):
    w_qkv, w_out, w_up, w_down, gain_rows, shift_rows, up_shift = weights
    slots, seq, width = hidden_part.shape
    heads = width // HEAD_DIM
    count = slots * seq
    qkv_shift = jnp.concatenate([shift_rows[0], jnp.zeros_like(shift_rows[0]), shift_rows[1]])
    key_mask = jnp.arange(seq)[None, :] < length_part[:, None]
    row_keep = key_mask.reshape(count, 1).astype(jnp.float32)
    hidden_in = hidden_part.reshape(count, width)
    hidden_low = hidden_in.astype(jnp.bfloat16)
    projected = jnp.dot(hidden_low, w_qkv, preferred_element_type=jnp.float32) + qkv_shift
    project_low = projected.astype(jnp.bfloat16).reshape(slots, seq, 3, heads, HEAD_DIM)
    queries = project_low[:, :, 0]
    key_rows = project_low[:, :, 1]
    value_rows = project_low[:, :, 2]
    scores = attend_scores(queries, key_rows, key_mask)
    row_max = jnp.max(scores, axis=-1, keepdims=True)
    raised = jnp.exp(scores - row_max)
    row_total = jnp.sum(raised, axis=-1, keepdims=True)
    probs = raised / row_total
    probs_low = probs.astype(jnp.bfloat16)
    mixed = jnp.einsum("shqk,skhd->sqhd", probs_low, value_rows, preferred_element_type=jnp.float32)
    mixed_low = mixed.reshape(count, width).astype(jnp.bfloat16)
    branch = jnp.dot(mixed_low, w_out, preferred_element_type=jnp.float32) + shift_rows[2]
    normed, first_back = jax.vjp(layer_norm, hidden_in + branch, gain_rows[0], shift_rows[4])
    normed_low = normed.astype(jnp.bfloat16)
    inner = jnp.dot(normed_low, w_up, preferred_element_type=jnp.float32) + up_shift
    active, gelu_back = jax.vjp(gelu_exact, inner)
    active_low = active.astype(jnp.bfloat16)
    feed = jnp.dot(active_low, w_down, preferred_element_type=jnp.float32) + shift_rows[3]
    final, second_back = jax.vjp(layer_norm, normed + feed, gain_rows[1], shift_rows[5])
    output = (final * row_keep).astype(jnp.bfloat16).reshape(slots, seq, width)
    grad_final = cot_part.reshape(count, width).astype(jnp.float32) * row_keep
    grad_h2, grad_gain_two, grad_shift_two = second_back(grad_final)
    grad_feed = grad_h2.astype(jnp.bfloat16)
    grad_down = jnp.einsum("rf,rd->fd", active_low, grad_feed, preferred_element_type=jnp.float32)
    grad_down_shift = jnp.sum(grad_feed, axis=0, dtype=jnp.float32)
    grad_active = jnp.einsum("rd,fd->rf", grad_feed, w_down, preferred_element_type=jnp.float32)
    grad_inner = gelu_back(grad_active)[0].astype(jnp.bfloat16)
    grad_up = jnp.einsum("rd,rf->df", normed_low, grad_inner, preferred_element_type=jnp.float32)
    grad_up_shift = jnp.sum(grad_inner, axis=0, dtype=jnp.float32)
    grad_normed = grad_h2 + jnp.einsum(
        "rf,df->rd", grad_inner, w_up, preferred_element_type=jnp.float32
    )
    grad_h, grad_gain_one, grad_shift_one = first_back(grad_normed)
    grad_branch = grad_h.astype(jnp.bfloat16)
    grad_out = jnp.einsum("rd,re->de", mixed_low, grad_branch, preferred_element_type=jnp.float32)
    grad_out_shift = jnp.sum(grad_branch, axis=0, dtype=jnp.float32)
    grad_mixed = jnp.einsum("re,de->rd", grad_branch, w_out, preferred_element_type=jnp.float32)
    grad_mixed_low = grad_mixed.astype(jnp.bfloat16).reshape(slots, seq, heads, HEAD_DIM)
    grad_probs = jnp.einsum(
        "sqhd,skhd->shqk", grad_mixed_low, value_rows, preferred_element_type=jnp.float32
    )
    row_dot = jnp.sum(probs * grad_probs, axis=-1, keepdims=True)
    grad_scores = (probs * (grad_probs - row_dot)).astype(jnp.bfloat16)
    grad_queries = (
        jnp.einsum("shqk,skhd->sqhd", grad_scores, key_rows, preferred_element_type=jnp.float32)
        * 0.125
    )
    grad_keys = (
        jnp.einsum("shqk,sqhd->skhd", grad_scores, queries, preferred_element_type=jnp.float32)
        * 0.125
    )
    grad_values = jnp.einsum(
        "shqk,sqhd->skhd", probs_low, grad_mixed_low, preferred_element_type=jnp.float32
    )
    grad_project = jnp.concatenate(
        [
            grad_queries.reshape(count, width).astype(jnp.bfloat16),
            grad_keys.reshape(count, width).astype(jnp.bfloat16),
            grad_values.reshape(count, width).astype(jnp.bfloat16),
        ],
        axis=1,
    )
    grad_qkv = jnp.einsum("rd,re->de", hidden_low, grad_project, preferred_element_type=jnp.float32)
    project_sums = jnp.sum(grad_project, axis=0, dtype=jnp.float32)
    grad_input = grad_h + jnp.einsum(
        "re,de->rd", grad_project, w_qkv, preferred_element_type=jnp.float32
    )
    small = jnp.stack(
        [
            grad_gain_one,
            grad_gain_two,
            project_sums[:width],
            project_sums[2 * width :],
            grad_out_shift,
            grad_down_shift,
            grad_shift_one,
            grad_shift_two,
        ]
    )
    return (output, grad_input.reshape(slots, seq, width), grad_qkv, grad_out, grad_up, grad_down, small, grad_up_shift)


def one_hot(places, size):
    return (places[:, None] == jnp.arange(size, dtype=jnp.int32)[None, :]).astype(jnp.bfloat16)


def local(
    expr,
    gene_owner,
    gene_row,
    lengths,
    cotangent,
    tables,
    w_qkv,
    w_out,
    w_up,
    w_down,
    gains,
    biases,
    up_bias,
):
    grid = Grid()
    micro, seq, width = expr.shape
    tok = micro * seq
    n_dp, n_table = lax.axis_size("dp"), lax.axis_size("table")
    group = n_table * tok
    capacity = 6 * tok // n_dp
    half = capacity // 2
    rows_dev = tables.shape[1]
    me_dp = lax.axis_index("dp")
    me_table = lax.axis_index("table")
    low = jnp.bfloat16

    part_rows = w_qkv.shape[0]
    up_cols = up_bias.shape[0] // part_rows
    small_cols = 8 + up_cols
    small = jnp.concatenate(
        [gains.T, biases.T, up_bias.reshape(up_cols, part_rows).T], axis=1
    )
    small = jnp.pad(small, ((0, 0), (0, 128 - small_cols)))
    shard_one = jnp.concatenate([w_qkv, w_out, small], axis=1)

    ids = gene_owner.reshape(tok) * rows_dev + gene_row.reshape(tok)
    all_ids = lax.all_gather(ids, AXES, axis=0, tiled=True).reshape(n_dp, group)
    all_owner = all_ids // rows_dev
    all_row = all_ids - all_owner * rows_dev
    mine = all_owner == me_dp
    ranks = jnp.cumsum(mine.astype(jnp.int32), axis=1) - 1
    match = mine[:, None, :] & (ranks[:, None, :] == jnp.arange(capacity, dtype=jnp.int32)[None, :, None])
    asked = jnp.sum(jnp.where(match, all_row[:, None, :], 0), axis=2)

    group_owner = pick(all_owner, me_dp, 0)
    hits = (group_owner[:, None] == jnp.arange(n_dp, dtype=jnp.int32)[None, :]).astype(jnp.int32)
    earlier = jnp.cumsum(hits, axis=0) - hits
    slot_index = jnp.sum(earlier * hits, axis=1)
    in_own = (slot_index // half) == grid.core
    place = jnp.where(in_own, 0, n_dp * half) + group_owner * half + slot_index % half
    place_dev = place.reshape(n_table, tok)

    found = jnp.take(tables[0], asked.reshape(-1), axis=0).reshape(n_dp, 2, half, width)
    sent = grid.swap(pick(found, 1 - grid.core, 1), grid.bit_core)
    pair = (pick(found, grid.core, 1).astype(jnp.float32) + sent.astype(jnp.float32)).astype(low)
    returned = lax.all_to_all(pair, "dp", split_axis=0, concat_axis=0, tiled=True)
    returned_other = grid.swap(returned, grid.bit_core)
    slots_all = jnp.concatenate(
        [returned.reshape(n_dp * half, width), returned_other.reshape(n_dp * half, width)]
    )
    own_place = pick(place_dev, me_table, 0)
    far_place = pick(place_dev, me_table ^ grid.bit_x, 0)
    far = jnp.dot(one_hot(far_place, 2 * n_dp * half), slots_all, preferred_element_type=jnp.float32)
    near = jnp.dot(one_hot(own_place, 2 * n_dp * half), slots_all, preferred_element_type=jnp.float32)
    embedded = near + grid.swap(far.astype(low), grid.bit_x).astype(jnp.float32)
    hidden = expr.astype(jnp.float32) + embedded.reshape(micro, seq, width)

    one = gather_chunk(grid, shard_one, True).reshape(grid.count * part_rows, -1)
    two = gather_chunk(grid, w_up, False).reshape(grid.count * part_rows, -1)
    full_down = gather_chunk(grid, w_down, True).reshape(grid.count * w_down.shape[0], -1)
    wide = w_qkv.shape[1]
    small_all = one[:, wide + width :].astype(jnp.float32)
    gain_rows = small_all[:, :2].T
    bias_rows = small_all[:, 2:8].T
    up_all = (
        small_all[:, 8:small_cols].reshape(grid.count, part_rows, up_cols).transpose(0, 2, 1).reshape(-1)
    )
    weights = (one[:, :wide], one[:, wide : wide + width], two, full_down, gain_rows, bias_rows, up_all)
    out, grad_expr, grad_qkv, grad_out, grad_up, grad_down, grad_small, grad_up_bias = layer_pass(
        weights, hidden, cotangent, lengths
    )

    sum_down = scatter_chunk(grid, grad_down, True)
    sum_up = scatter_chunk(grid, grad_up, False)
    small_cat = jnp.concatenate(
        [
            grad_small.T,
            grad_up_bias.reshape(grid.count, up_cols, part_rows).transpose(0, 2, 1).reshape(-1, up_cols),
        ],
        axis=1,
    )
    small_cat = jnp.pad(small_cat, ((0, 0), (0, 128 - small_cols)))
    sum_one = scatter_chunk(grid, jnp.concatenate([grad_qkv, grad_out, small_cat], axis=1), True)
    sum_small = sum_one[:, wide + width :]

    flat = grad_expr.reshape(tok, width).astype(low)
    flat_x = grid.swap(flat, grid.bit_x)
    flat_c = grid.swap(flat, grid.bit_core)
    flat_xc = grid.swap(flat_x, grid.bit_core)
    group_grads = jnp.concatenate([flat, flat_c, flat_x, flat_xc])
    places = jnp.concatenate([pick(place_dev, me_table ^ step, 0) for step in range(n_table)])
    choose = (jnp.arange(n_dp * half, dtype=jnp.int32)[:, None] == places[None, :]).astype(low)
    outgoing = jnp.dot(choose, group_grads, preferred_element_type=jnp.float32).astype(low)
    incoming = lax.all_to_all(
        outgoing.reshape(n_dp, half, width), "dp", split_axis=0, concat_axis=0, tiled=True
    )
    incoming_other = grid.swap(incoming, grid.bit_core)
    arrived = ordered(grid.core, incoming, incoming_other, 1).reshape(n_dp * capacity, width)
    table_grad = jax.ops.segment_sum(
        arrived.astype(jnp.float32), asked.reshape(-1), num_segments=rows_dev
    )
    return (
        out,
        grad_expr,
        table_grad[None],
        sum_one[:, :wide],
        sum_one[:, wide : wide + width],
        sum_up,
        sum_down,
        sum_small[:, :2].T,
        sum_small[:, 2:8].T,
        sum_small[:, 8:small_cols].T.reshape(-1),
    )


def solution(mesh):
    both = ("dp", "table")
    placed = (
        P(both, None, None),
        P(both, None, None),
        P(both, None),
        P(both),
        P(both, None, None),
        P("table", "dp", None),
        P(both, None),
        P(both, None),
        P(both, None),
        P(both, None),
        P(None, both),
        P(None, both),
        P(both),
    )
    return jax.shard_map(
        local,
        mesh=mesh,
        in_specs=placed,
        out_specs=(
            P(both, None, None),
            P(both, None, None),
            P("table", "dp", None),
            P(both, None),
            P(both, None),
            P(both, None),
            P(both, None),
            P(None, both),
            P(None, both),
            P(both),
        ),
        check_vma=False,
    )
```

```python
import functools

import jax
import jax.numpy as jnp
from jax import lax
from jax.experimental import pallas as pl
from jax.experimental.pallas import tpu as pltpu
from jax.sharding import PartitionSpec as P

HEAD_DIM = 64
AXES = ("dp", "table")


LOW = jnp.bfloat16
F32 = jnp.float32
MESH = pl.DeviceIdType.MESH


def dot(left, right):
    return jnp.dot(left, right, preferred_element_type=F32)


class Net:
    def __init__(self, send_sems, recv_sems):
        self.dp, self.table = lax.axis_index("dp"), lax.axis_index("table")
        self.z, self.y = self.dp // 2, self.dp % 2
        self.x, self.c = self.table // 2, self.table % 2
        self.line = (self.z, self.z + 1 - 2 * (self.z % 2), (self.z + 2) % 4, 3 - self.z)
        self.send_sems, self.recv_sems = send_sems, recv_sems
        self.used = 0
        self.open = []

    def at(self, z=None, y=None, x=None, c=None):
        z = self.z if z is None else z
        y = self.y if y is None else y
        x = self.x if x is None else x
        c = self.c if c is None else c
        return (z * 2 + y, x * 2 + c)

    def send(self, source, target, device):
        copy = pltpu.make_async_remote_copy(
            src_ref=source,
            dst_ref=target,
            send_sem=self.send_sems.at[self.used],
            recv_sem=self.recv_sems.at[self.used],
            device_id=device,
            device_id_type=MESH,
        )
        self.used += 1
        copy.start()
        self.open.append(copy)
        return copy

    def close(self):
        for copy in self.open:
            copy.wait_send()

    def across_x(self):
        return self.at(x=1 - self.x)

    def across_y(self):
        return self.at(y=1 - self.y)

    def across_c(self):
        return self.at(c=1 - self.c)

    def greet_all(self):
        barrier = pltpu.get_barrier_semaphore()
        me = self.dp * 4 + self.table
        for step in range(1, 32):
            other = (me + step) % 32
            pl.semaphore_signal(
                barrier, inc=1, device_id=(other // 4, other % 4), device_id_type=MESH
            )
        pl.semaphore_wait(barrier, 31)


class Spread:
    def __init__(self, net, shard, whole, split):
        self.net, self.shard, self.whole = net, shard, whole
        cols = shard.shape[1]
        self.first, self.second = pl.ds(0, split), pl.ds(split, cols - split)

    def start_line(self):
        net = self.net
        mine = self.whole.at[net.z, net.y, net.x, net.c]
        self.from_z = [None] + [
            net.send(self.shard, mine, net.at(z=net.line[step])) for step in (1, 2, 3)
        ]

    def start_sides(self):
        net = self.net
        mine = self.whole.at[net.z, net.y, net.x, net.c]
        self.from_x = [net.send(self.shard, mine, net.across_x())]
        self.from_y = [net.send(self.shard, mine, net.across_y())]

    def sides(self):
        net = self.net
        for step in (1, 2, 3):
            self.from_z[step].wait_recv()
            part = self.whole.at[net.line[step], net.y, net.x, net.c]
            self.from_x.append(net.send(part, part, net.across_x()))
            self.from_y.append(net.send(part, part, net.across_y()))

    def corners(self):
        net = self.net
        self.from_corner = []
        for step in range(4):
            self.from_x[step].wait_recv()
            part = self.whole.at[net.line[step], net.y, 1 - net.x, net.c, :, self.first]
            self.from_corner.append(net.send(part, part, net.across_y()))
            self.from_y[step].wait_recv()
            part = self.whole.at[net.line[step], 1 - net.y, net.x, net.c, :, self.second]
            self.from_corner.append(net.send(part, part, net.across_x()))

    def cores(self):
        net = self.net
        self.from_core = []
        self.kept.wait()
        for y, x in ((net.y, net.x), (net.y, 1 - net.x), (1 - net.y, net.x)):
            part = self.whole.at[:, y, x, net.c]
            self.from_core.append(net.send(part, part, net.across_c()))
        for copy in self.from_corner:
            copy.wait_recv()
        part = self.whole.at[:, 1 - net.y, 1 - net.x, net.c]
        self.from_core.append(net.send(part, part, net.across_c()))

    def finish(self):
        for copy in self.from_core:
            copy.wait_recv()


def ranks_of(mask, before, below):
    marks = mask.astype(LOW)
    within = dot(marks, before)
    rows = dot(marks, jnp.ones((128, 128), LOW))
    return within + dot(below, rows.astype(LOW))


def fetch_kernel(
    row_bits,
    capacity,
    ids_ref,
    expr_ref,
    table_ref,
    shard_one,
    shard_up,
    shard_down,
    hidden_ref,
    place_ref,
    asked_ref,
    whole_one,
    whole_up,
    whole_down,
    all_ids,
    grouped,
    rank_ref,
    rows_ref,
    place_dev,
    rows_table,
    chosen,
    found,
    partner,
    pair,
    owned,
    owned_far,
    picks,
    far,
    far_in,
    send_sems,
    recv_sems,
    local_sems,
):
    net = Net(send_sems, recv_sems)
    half = capacity // 2
    rows_dev, width = table_ref.shape
    table_copy = pltpu.make_async_copy(table_ref, rows_table, local_sems.at[0])
    table_copy.start()
    spreads = [
        Spread(net, shard_one, whole_one, 1664),
        Spread(net, shard_up, whole_up, 1536),
        Spread(net, shard_down, whole_down, 384),
    ]
    for index, spread in enumerate(spreads):
        copy = pltpu.make_async_copy(
            spread.shard, spread.whole.at[net.z, net.y, net.x, net.c], local_sems.at[1 + index]
        )
        copy.start()
        spread.kept = copy
    net.greet_all()
    me = net.dp * 4 + net.table
    all_ids[me] = ids_ref[...]
    ids_in = []
    for step in range(1, 32):
        other = (me + step) % 32
        ids_in.append(net.send(ids_ref, all_ids.at[me], (other // 4, other % 4)))
    spreads[0].start_line()
    spreads[0].start_sides()
    spreads[1].start_line()
    spreads[1].start_sides()
    spreads[2].start_sides()
    for copy in ids_in:
        copy.wait_recv()
    for group in range(8):
        for table in range(4):
            grouped[group, pl.ds(2 * table, 2), :] = all_ids[4 * group + table]

    lanes = lax.broadcasted_iota(jnp.int32, (128, 128), 1)
    subs = lax.broadcasted_iota(jnp.int32, (128, 128), 0)
    before = (subs < lanes).astype(LOW)
    low_sub = lax.broadcasted_iota(jnp.int32, (64, 64), 0)
    low_lane = lax.broadcasted_iota(jnp.int32, (64, 64), 1)
    below = ((low_lane < low_sub) & (low_lane // 8 == low_sub // 8)).astype(LOW)
    every = grouped[...].reshape(64, 128)
    owner = lax.shift_right_logical(every, row_bits)
    rows_ref[...] = jnp.bitwise_and(every, (1 << row_bits) - 1).astype(F32)
    mine = (owner == net.dp).astype(F32)
    rank_ref[...] = jnp.where(mine > 0, ranks_of(mine, before, below), -1.0)

    slot_sub = lax.broadcasted_iota(jnp.int32, (capacity, 128), 0).astype(F32)
    lane_row = lax.broadcasted_iota(jnp.int32, (capacity, 128), 1).astype(F32)

    def choose(step, base):
        group = (net.dp + step) % 8

        def gather_row(row, total):
            rank = rank_ref[pl.ds(group * 8 + row, 1), :]
            value = rows_ref[pl.ds(group * 8 + row, 1), :]
            return total + jnp.where(slot_sub == rank, value, 0.0)

        total = lax.fori_loop(0, 8, gather_row, jnp.zeros((capacity, 128), F32))
        column = jnp.broadcast_to(jnp.sum(total, axis=1, keepdims=True), (capacity, 128))
        asked_ref[group] = jnp.transpose(column)[0:8, :]
        start = pl.multiple_of((step - base) * capacity, 8)

        def mark(block, carry):
            at = pl.multiple_of(block * 128, 128)
            hit = column == lane_row + (block * 128).astype(F32)
            chosen[pl.ds(start, capacity), pl.ds(at, 128)] = jnp.where(hit, 1.0, 0.0).astype(LOW)
            return carry

        lax.fori_loop(0, rows_dev // 128, mark, 0)

    def look_up(base):
        lax.fori_loop(base, base + 4, lambda step, carry: (choose(step, base), carry)[1], 0)

        def columns(block, carry):
            at = pl.multiple_of(block * 256, 256)
            value = dot(chosen[...], rows_table[:, pl.ds(at, 256)]).astype(LOW)
            found[pl.ds(base, 4), :, :, pl.ds(at, 256)] = value.reshape(4, 2, half, 256)
            return carry

        lax.fori_loop(0, width // 256, columns, 0)

    def add_pairs(base):
        for step in range(base, base + 4):
            mine_half = found[step, net.c].astype(F32)
            pair[pl.ds(step * half, half), :] = (mine_half + partner[step].astype(F32)).astype(LOW)

    table_copy.wait()
    look_up(0)
    pair_in = [net.send(found.at[pl.ds(0, 4), 1 - net.c], partner.at[pl.ds(0, 4)], net.across_c())]
    look_up(4)
    pair_in.append(
        net.send(found.at[pl.ds(4, 4), 1 - net.c], partner.at[pl.ds(4, 4)], net.across_c())
    )
    here = pl.ds(pl.multiple_of(net.dp * half, 8), half)
    rows_in = []
    for base in (0, 4):
        pair_in[base // 4].wait_recv()
        add_pairs(base)
        for step in range(base, base + 4):
            if step == 0:
                owned[here, :] = pair[pl.ds(0, half), :]
                continue
            other = (net.dp + step) % 8
            rows_in.append(
                net.send(pair.at[pl.ds(step * half, half), :], owned.at[here, :], (other, net.table))
            )
    spreads[2].start_line()
    spreads[0].sides()
    spreads[0].corners()

    hits_owner = lax.shift_right_logical(grouped[net.dp], row_bits).astype(F32)
    owners = lax.broadcasted_iota(jnp.int32, (8, 8, 128), 0).astype(F32)
    hits = (hits_owner[None] == owners).astype(F32).reshape(64, 128)
    slot = jnp.sum((ranks_of(hits, before, below) * hits).reshape(8, 8, 128), axis=0)
    upper = (slot >= half).astype(F32)
    away = jnp.where(upper == net.c.astype(F32), 0.0, 8.0 * half)
    place = hits_owner * half + slot - upper * half + away
    place_ref[...] = place
    for table in range(4):
        place_dev[table] = place[2 * table : 2 * table + 2]
    wide_lane = lax.broadcasted_iota(jnp.int32, (128, 128), 1).astype(F32)

    def spread_marks(table, base):
        for row in range(2):
            line = place_dev[table, pl.ds(row, 1), :]
            column = jnp.transpose(jnp.broadcast_to(line, (128, 128)))

            def mark(block, carry):
                at = pl.multiple_of(block * 128, 128)
                hit = column == wide_lane + (block * 128).astype(F32)
                picks[pl.ds(base + 128 * row, 128), pl.ds(at, 128)] = jnp.where(hit, 1.0, 0.0).astype(LOW)
                return carry

            lax.fori_loop(0, 16 * half // 128, mark, 0)

    spread_marks(net.table, 0)
    spread_marks((1 - net.x) * 2 + net.c, 256)
    for copy in rows_in:
        copy.wait_recv()
    owned_in = net.send(owned, owned_far, net.across_c())
    owned_in.wait_recv()

    def select(base):
        marks = picks[pl.ds(base, 256), :]
        return dot(marks[:, : 8 * half], owned[...]) + dot(marks[:, 8 * half :], owned_far[...])

    far[...] = select(256).astype(LOW)
    far_copy = net.send(far, far_in, net.across_x())
    near = select(0) + expr_ref[...].astype(F32)
    spreads[1].sides()
    spreads[1].corners()
    spreads[0].cores()
    far_copy.wait_recv()
    hidden_ref[...] = near + far_in[...].astype(F32)
    spreads[2].sides()
    spreads[2].corners()
    spreads[1].cores()
    spreads[2].cores()
    for spread in spreads:
        spread.finish()
    net.close()


def fetch(ids, expr, table, shard_one, shard_up, shard_down, row_bits, capacity):
    tok, width = expr.shape
    half = capacity // 2
    rows_dev = table.shape[0]
    vmem = pl.BlockSpec(memory_space=pltpu.VMEM)
    hbm = pl.BlockSpec(memory_space=pl.ANY)

    def whole(shard):
        return jax.ShapeDtypeStruct((4, 2, 2, 2) + shard.shape, LOW)

    count = 31 + 3 * 23 + 2 + 7 + 2
    return pl.pallas_call(
        functools.partial(fetch_kernel, row_bits, capacity),
        out_shape=(
            jax.ShapeDtypeStruct((tok, width), F32),
            jax.ShapeDtypeStruct((8, 128), F32),
            jax.ShapeDtypeStruct((8, 8, capacity), F32),
            whole(shard_one),
            whole(shard_up),
            whole(shard_down),
        ),
        in_specs=[vmem, vmem, hbm, hbm, hbm, hbm],
        out_specs=(vmem, vmem, vmem, hbm, hbm, hbm),
        scratch_shapes=[
            pltpu.VMEM((32, 2, 128), jnp.int32),
            pltpu.VMEM((8, 8, 128), jnp.int32),
            pltpu.VMEM((64, 128), F32),
            pltpu.VMEM((64, 128), F32),
            pltpu.VMEM((4, 2, 128), F32),
            pltpu.VMEM((rows_dev, width), LOW),
            pltpu.VMEM((4 * capacity, rows_dev), LOW),
            pltpu.VMEM((8, 2, half, width), LOW),
            pltpu.VMEM((8, half, width), LOW),
            pltpu.VMEM((8 * half, width), LOW),
            pltpu.VMEM((8 * half, width), LOW),
            pltpu.VMEM((8 * half, width), LOW),
            pltpu.VMEM((2 * tok, 16 * half), LOW),
            pltpu.VMEM((tok, width), LOW),
            pltpu.VMEM((tok, width), LOW),
            pltpu.SemaphoreType.DMA((count,)),
            pltpu.SemaphoreType.DMA((count,)),
            pltpu.SemaphoreType.DMA((4,)),
        ],
        compiler_params=pltpu.CompilerParams(
            collective_id=0, has_side_effects=True, vmem_limit_bytes=60 * 2**20
        ),
        name="fetch",
    )(ids, expr, table, shard_one, shard_up, shard_down)


def layer_norm(values, scale, shift):
    center = values - jnp.mean(values, axis=-1, keepdims=True)
    spread = jnp.mean(center * center, axis=-1, keepdims=True)
    return center * lax.rsqrt(spread + 1e-05) * scale + shift


def gelu_exact(values):
    return jax.nn.gelu(values, approximate=False)


class Grid:
    def __init__(self):
        dp, table = lax.axis_size("dp"), lax.axis_size("table")
        self.count = dp * table
        self.high = dp // 2
        self.side = table // 2
        self.bit_core = 1
        self.bit_x = 2
        self.bit_y = table
        self.bit_z = 2 * table
        me_dp, me_table = lax.axis_index("dp"), lax.axis_index("table")
        self.z, self.y = me_dp // 2, me_dp % 2
        self.x, self.core = me_table // 2, me_table % 2

    def swap(self, value, mask):
        pairs = [(index, index ^ mask) for index in range(self.count)]
        return lax.ppermute(value, AXES, pairs)


def ordered(flag, own, other, axis):
    first = flag == 0
    return jnp.stack([jnp.where(first, own, other), jnp.where(first, other, own)], axis=axis)


def pick(values, index, axis):
    return lax.dynamic_index_in_dim(values, index, axis=axis, keepdims=False)


def gather_chunk(grid, shard, x_first):
    rows = [shard] + [grid.swap(shard, grid.bit_z * step) for step in range(1, grid.high)]
    line = jnp.stack(rows)
    place = jnp.arange(grid.high) ^ grid.z
    line = jnp.stack(
        [
            sum_select([(place[spot] == step, rows[step]) for step in range(grid.high)])
            for spot in range(grid.high)
        ]
    )
    first, second = (grid.bit_x, grid.bit_y) if x_first else (grid.bit_y, grid.bit_x)
    one = grid.swap(line, first)
    two = grid.swap(line, second)
    three = grid.swap(one, second)
    if x_first:
        own_y, other_y = ordered(grid.x, line, one, 1), ordered(grid.x, two, three, 1)
        plane = ordered(grid.y, own_y, other_y, 1)
    else:
        own_x, other_x = ordered(grid.y, line, one, 1), ordered(grid.y, two, three, 1)
        plane = ordered(grid.x, own_x, other_x, 2)
    partner = grid.swap(plane, grid.bit_core)
    whole = ordered(grid.core, plane, partner, 3)
    return whole.reshape((grid.count,) + shard.shape)


def sum_select(choices):
    result = choices[-1][1]
    for test, value in choices[:-1]:
        result = jnp.where(test, value, result)
    return result


def scatter_chunk(grid, grads, x_first):
    rows = grads.shape[0] // grid.count
    blocks = grads.reshape((grid.high, 2, grid.side, 2, rows, grads.shape[1]))
    low = jnp.bfloat16

    def halve(value, flag, axis, bit):
        sent = grid.swap(pick(value, 1 - flag, axis).astype(low), bit)
        return pick(value, flag, axis).astype(jnp.float32) + sent.astype(jnp.float32)

    part = halve(blocks, grid.core, 3, grid.bit_core).astype(low)
    if x_first:
        part = halve(part, grid.x, 2, grid.bit_x).astype(low)
        part = halve(part, grid.y, 1, grid.bit_y).astype(low)
    else:
        part = halve(part, grid.y, 1, grid.bit_y).astype(low)
        part = halve(part, grid.x, 1, grid.bit_x).astype(low)
    total = pick(part, grid.z, 0).astype(jnp.float32)
    for step in range(1, grid.high):
        total = total + grid.swap(pick(part, grid.z ^ step, 0), grid.bit_z * step).astype(jnp.float32)
    return total


def attend_scores(queries, key_rows, key_mask):
    scores = (
        jnp.einsum("sqhd,skhd->shqk", queries, key_rows, preferred_element_type=jnp.float32) * 0.125
    )
    return jnp.where(key_mask[:, None, None, :], scores, -1e30)


def layer_pass(weights, hidden_part, cot_part, length_part):
    w_qkv, w_out, w_up, w_down, gain_rows, shift_rows, up_shift = weights
    slots, seq, width = hidden_part.shape
    heads = width // HEAD_DIM
    count = slots * seq
    qkv_shift = jnp.concatenate([shift_rows[0], jnp.zeros_like(shift_rows[0]), shift_rows[1]])
    key_mask = jnp.arange(seq)[None, :] < length_part[:, None]
    row_keep = key_mask.reshape(count, 1).astype(jnp.float32)
    hidden_in = hidden_part.reshape(count, width)
    hidden_low = hidden_in.astype(jnp.bfloat16)
    projected = jnp.dot(hidden_low, w_qkv, preferred_element_type=jnp.float32) + qkv_shift
    project_low = projected.astype(jnp.bfloat16).reshape(slots, seq, 3, heads, HEAD_DIM)
    queries = project_low[:, :, 0]
    key_rows = project_low[:, :, 1]
    value_rows = project_low[:, :, 2]
    scores = attend_scores(queries, key_rows, key_mask)
    row_max = jnp.max(scores, axis=-1, keepdims=True)
    raised = jnp.exp(scores - row_max)
    row_total = jnp.sum(raised, axis=-1, keepdims=True)
    probs = raised / row_total
    probs_low = probs.astype(jnp.bfloat16)
    mixed = jnp.einsum("shqk,skhd->sqhd", probs_low, value_rows, preferred_element_type=jnp.float32)
    mixed_low = mixed.reshape(count, width).astype(jnp.bfloat16)
    branch = jnp.dot(mixed_low, w_out, preferred_element_type=jnp.float32) + shift_rows[2]
    normed, first_back = jax.vjp(layer_norm, hidden_in + branch, gain_rows[0], shift_rows[4])
    normed_low = normed.astype(jnp.bfloat16)
    inner = jnp.dot(normed_low, w_up, preferred_element_type=jnp.float32) + up_shift
    active, gelu_back = jax.vjp(gelu_exact, inner)
    active_low = active.astype(jnp.bfloat16)
    feed = jnp.dot(active_low, w_down, preferred_element_type=jnp.float32) + shift_rows[3]
    final, second_back = jax.vjp(layer_norm, normed + feed, gain_rows[1], shift_rows[5])
    output = (final * row_keep).astype(jnp.bfloat16).reshape(slots, seq, width)
    grad_final = cot_part.reshape(count, width).astype(jnp.float32) * row_keep
    grad_h2, grad_gain_two, grad_shift_two = second_back(grad_final)
    grad_feed = grad_h2.astype(jnp.bfloat16)
    grad_down = jnp.einsum("rf,rd->fd", active_low, grad_feed, preferred_element_type=jnp.float32)
    grad_down_shift = jnp.sum(grad_feed, axis=0, dtype=jnp.float32)
    grad_active = jnp.einsum("rd,fd->rf", grad_feed, w_down, preferred_element_type=jnp.float32)
    grad_inner = gelu_back(grad_active)[0].astype(jnp.bfloat16)
    grad_up = jnp.einsum("rd,rf->df", normed_low, grad_inner, preferred_element_type=jnp.float32)
    grad_up_shift = jnp.sum(grad_inner, axis=0, dtype=jnp.float32)
    grad_normed = grad_h2 + jnp.einsum(
        "rf,df->rd", grad_inner, w_up, preferred_element_type=jnp.float32
    )
    grad_h, grad_gain_one, grad_shift_one = first_back(grad_normed)
    grad_branch = grad_h.astype(jnp.bfloat16)
    grad_out = jnp.einsum("rd,re->de", mixed_low, grad_branch, preferred_element_type=jnp.float32)
    grad_out_shift = jnp.sum(grad_branch, axis=0, dtype=jnp.float32)
    grad_mixed = jnp.einsum("re,de->rd", grad_branch, w_out, preferred_element_type=jnp.float32)
    grad_mixed_low = grad_mixed.astype(jnp.bfloat16).reshape(slots, seq, heads, HEAD_DIM)
    grad_probs = jnp.einsum(
        "sqhd,skhd->shqk", grad_mixed_low, value_rows, preferred_element_type=jnp.float32
    )
    row_dot = jnp.sum(probs * grad_probs, axis=-1, keepdims=True)
    grad_scores = (probs * (grad_probs - row_dot)).astype(jnp.bfloat16)
    grad_queries = (
        jnp.einsum("shqk,skhd->sqhd", grad_scores, key_rows, preferred_element_type=jnp.float32)
        * 0.125
    )
    grad_keys = (
        jnp.einsum("shqk,sqhd->skhd", grad_scores, queries, preferred_element_type=jnp.float32)
        * 0.125
    )
    grad_values = jnp.einsum(
        "shqk,sqhd->skhd", probs_low, grad_mixed_low, preferred_element_type=jnp.float32
    )
    grad_project = jnp.concatenate(
        [
            grad_queries.reshape(count, width).astype(jnp.bfloat16),
            grad_keys.reshape(count, width).astype(jnp.bfloat16),
            grad_values.reshape(count, width).astype(jnp.bfloat16),
        ],
        axis=1,
    )
    grad_qkv = jnp.einsum("rd,re->de", hidden_low, grad_project, preferred_element_type=jnp.float32)
    project_sums = jnp.sum(grad_project, axis=0, dtype=jnp.float32)
    grad_input = grad_h + jnp.einsum(
        "re,de->rd", grad_project, w_qkv, preferred_element_type=jnp.float32
    )
    small = jnp.stack(
        [
            grad_gain_one,
            grad_gain_two,
            project_sums[:width],
            project_sums[2 * width :],
            grad_out_shift,
            grad_down_shift,
            grad_shift_one,
            grad_shift_two,
        ]
    )
    return (output, grad_input.reshape(slots, seq, width), grad_qkv, grad_out, grad_up, grad_down, small, grad_up_shift)


def one_hot(places, size):
    return (places[:, None] == jnp.arange(size, dtype=jnp.int32)[None, :]).astype(jnp.bfloat16)


def local(
    expr,
    gene_owner,
    gene_row,
    lengths,
    cotangent,
    tables,
    w_qkv,
    w_out,
    w_up,
    w_down,
    gains,
    biases,
    up_bias,
):
    grid = Grid()
    micro, seq, width = expr.shape
    tok = micro * seq
    n_dp, n_table = lax.axis_size("dp"), lax.axis_size("table")
    group = n_table * tok
    capacity = 6 * tok // n_dp
    half = capacity // 2
    rows_dev = tables.shape[1]
    me_dp = lax.axis_index("dp")
    me_table = lax.axis_index("table")
    low = jnp.bfloat16

    part_rows = w_qkv.shape[0]
    up_cols = up_bias.shape[0] // part_rows
    small_cols = 8 + up_cols
    small = jnp.concatenate(
        [gains.T, biases.T, up_bias.reshape(up_cols, part_rows).T], axis=1
    )
    small = jnp.pad(small, ((0, 0), (0, 128 - small_cols)))
    shard_one = jnp.concatenate([w_qkv, w_out, small], axis=1)

    fast = (n_dp, n_table, seq, micro, width) == (8, 4, 128, 2, 768) and rows_dev % 128 == 0
    if fast:
        row_bits = rows_dev.bit_length()
        ids = gene_owner.reshape(micro, seq) * (1 << row_bits) + gene_row
        hidden, place, asked, one, two, full_down = fetch(
            ids, expr.reshape(tok, width), tables[0], shard_one, w_up, w_down, row_bits, capacity
        )
        hidden = hidden.reshape(micro, seq, width)
        place_dev = place.astype(jnp.int32).reshape(n_table, tok)
        asked = asked[:, 0, :].astype(jnp.int32)
        return finish(grid, hidden, place_dev, asked, one, two, full_down, expr, tables, lengths, cotangent, w_qkv, w_down, up_cols)
    ids = gene_owner.reshape(tok) * rows_dev + gene_row.reshape(tok)
    all_ids = lax.all_gather(ids, AXES, axis=0, tiled=True).reshape(n_dp, group)
    all_owner = all_ids // rows_dev
    all_row = all_ids - all_owner * rows_dev
    mine = all_owner == me_dp
    ranks = jnp.cumsum(mine.astype(jnp.int32), axis=1) - 1
    match = mine[:, None, :] & (ranks[:, None, :] == jnp.arange(capacity, dtype=jnp.int32)[None, :, None])
    asked = jnp.sum(jnp.where(match, all_row[:, None, :], 0), axis=2)

    group_owner = pick(all_owner, me_dp, 0)
    hits = (group_owner[:, None] == jnp.arange(n_dp, dtype=jnp.int32)[None, :]).astype(jnp.int32)
    earlier = jnp.cumsum(hits, axis=0) - hits
    slot_index = jnp.sum(earlier * hits, axis=1)
    in_own = (slot_index // half) == grid.core
    place = jnp.where(in_own, 0, n_dp * half) + group_owner * half + slot_index % half
    place_dev = place.reshape(n_table, tok)

    found = jnp.take(tables[0], asked.reshape(-1), axis=0).reshape(n_dp, 2, half, width)
    sent = grid.swap(pick(found, 1 - grid.core, 1), grid.bit_core)
    pair = (pick(found, grid.core, 1).astype(jnp.float32) + sent.astype(jnp.float32)).astype(low)
    returned = lax.all_to_all(pair, "dp", split_axis=0, concat_axis=0, tiled=True)
    returned_other = grid.swap(returned, grid.bit_core)
    slots_all = jnp.concatenate(
        [returned.reshape(n_dp * half, width), returned_other.reshape(n_dp * half, width)]
    )
    own_place = pick(place_dev, me_table, 0)
    far_place = pick(place_dev, me_table ^ grid.bit_x, 0)
    far = jnp.dot(one_hot(far_place, 2 * n_dp * half), slots_all, preferred_element_type=jnp.float32)
    near = jnp.dot(one_hot(own_place, 2 * n_dp * half), slots_all, preferred_element_type=jnp.float32)
    embedded = near + grid.swap(far.astype(low), grid.bit_x).astype(jnp.float32)
    hidden = expr.astype(jnp.float32) + embedded.reshape(micro, seq, width)

    one = gather_chunk(grid, shard_one, True)
    two = gather_chunk(grid, w_up, False)
    full_down = gather_chunk(grid, w_down, True)
    return finish(grid, hidden, place_dev, asked, one, two, full_down, expr, tables, lengths, cotangent, w_qkv, w_down, up_cols)


def finish(grid, hidden, place_dev, asked, one, two, full_down, expr, tables, lengths, cotangent, w_qkv, w_down, up_cols):
    micro, seq, width = expr.shape
    tok = micro * seq
    n_dp, n_table = lax.axis_size("dp"), lax.axis_size("table")
    capacity = 6 * tok // n_dp
    half = capacity // 2
    rows_dev = tables.shape[1]
    me_table = lax.axis_index("table")
    low = jnp.bfloat16
    part_rows = w_qkv.shape[0]
    small_cols = 8 + up_cols
    one = one.reshape(grid.count * part_rows, -1)
    two = two.reshape(grid.count * part_rows, -1)
    full_down = full_down.reshape(grid.count * w_down.shape[0], -1)
    wide = w_qkv.shape[1]
    small_all = one[:, wide + width :].astype(jnp.float32)
    gain_rows = small_all[:, :2].T
    bias_rows = small_all[:, 2:8].T
    up_all = (
        small_all[:, 8:small_cols].reshape(grid.count, part_rows, up_cols).transpose(0, 2, 1).reshape(-1)
    )
    weights = (one[:, :wide], one[:, wide : wide + width], two, full_down, gain_rows, bias_rows, up_all)
    out, grad_expr, grad_qkv, grad_out, grad_up, grad_down, grad_small, grad_up_bias = layer_pass(
        weights, hidden, cotangent, lengths
    )

    sum_down = scatter_chunk(grid, grad_down, True)
    sum_up = scatter_chunk(grid, grad_up, False)
    small_cat = jnp.concatenate(
        [
            grad_small.T,
            grad_up_bias.reshape(grid.count, up_cols, part_rows).transpose(0, 2, 1).reshape(-1, up_cols),
        ],
        axis=1,
    )
    small_cat = jnp.pad(small_cat, ((0, 0), (0, 128 - small_cols)))
    sum_one = scatter_chunk(grid, jnp.concatenate([grad_qkv, grad_out, small_cat], axis=1), True)
    sum_small = sum_one[:, wide + width :]

    flat = grad_expr.reshape(tok, width).astype(low)
    flat_x = grid.swap(flat, grid.bit_x)
    flat_c = grid.swap(flat, grid.bit_core)
    flat_xc = grid.swap(flat_x, grid.bit_core)
    group_grads = jnp.concatenate([flat, flat_c, flat_x, flat_xc])
    places = jnp.concatenate([pick(place_dev, me_table ^ step, 0) for step in range(n_table)])
    choose = (jnp.arange(n_dp * half, dtype=jnp.int32)[:, None] == places[None, :]).astype(low)
    outgoing = jnp.dot(choose, group_grads, preferred_element_type=jnp.float32).astype(low)
    incoming = lax.all_to_all(
        outgoing.reshape(n_dp, half, width), "dp", split_axis=0, concat_axis=0, tiled=True
    )
    incoming_other = grid.swap(incoming, grid.bit_core)
    arrived = ordered(grid.core, incoming, incoming_other, 1).reshape(n_dp * capacity, width)
    table_grad = jax.ops.segment_sum(
        arrived.astype(jnp.float32), asked.reshape(-1), num_segments=rows_dev
    )
    return (
        out,
        grad_expr,
        table_grad[None],
        sum_one[:, :wide],
        sum_one[:, wide : wide + width],
        sum_up,
        sum_down,
        sum_small[:, :2].T,
        sum_small[:, 2:8].T,
        sum_small[:, 8:small_cols].T.reshape(-1),
    )


def solution(mesh):
    both = ("dp", "table")
    placed = (
        P(both, None, None),
        P(both, None, None),
        P(both, None),
        P(both),
        P(both, None, None),
        P("table", "dp", None),
        P(both, None),
        P(both, None),
        P(both, None),
        P(both, None),
        P(None, both),
        P(None, both),
        P(both),
    )
    return jax.shard_map(
        local,
        mesh=mesh,
        in_specs=placed,
        out_specs=(
            P(both, None, None),
            P(both, None, None),
            P("table", "dp", None),
            P(both, None),
            P(both, None),
            P(both, None),
            P(both, None),
            P(None, both),
            P(None, both),
            P(both),
        ),
        check_vma=False,
    )
```

```python
import functools

import jax
import jax.numpy as jnp
from jax import lax
from jax.experimental import pallas as pl
from jax.experimental.pallas import tpu as pltpu
from jax.sharding import PartitionSpec as P

HEAD_DIM = 64
AXES = ("dp", "table")


LOW = jnp.bfloat16
F32 = jnp.float32
MESH = pl.DeviceIdType.MESH


def dot(left, right):
    return jnp.dot(left, right, preferred_element_type=F32)


class Net:
    def __init__(self, send_sems, recv_sems):
        self.dp, self.table = lax.axis_index("dp"), lax.axis_index("table")
        self.z, self.y = self.dp // 2, self.dp % 2
        self.x, self.c = self.table // 2, self.table % 2
        self.line = (self.z, self.z + 1 - 2 * (self.z % 2), (self.z + 2) % 4, 3 - self.z)
        self.send_sems, self.recv_sems = send_sems, recv_sems
        self.used = 0
        self.open = []

    def at(self, z=None, y=None, x=None, c=None):
        z = self.z if z is None else z
        y = self.y if y is None else y
        x = self.x if x is None else x
        c = self.c if c is None else c
        return (z * 2 + y, x * 2 + c)

    def send(self, source, target, device):
        copy = pltpu.make_async_remote_copy(
            src_ref=source,
            dst_ref=target,
            send_sem=self.send_sems.at[self.used],
            recv_sem=self.recv_sems.at[self.used],
            device_id=device,
            device_id_type=MESH,
        )
        self.used += 1
        copy.start()
        self.open.append(copy)
        return copy

    def close(self):
        for copy in self.open:
            copy.wait_send()

    def across_x(self):
        return self.at(x=1 - self.x)

    def across_y(self):
        return self.at(y=1 - self.y)

    def across_c(self):
        return self.at(c=1 - self.c)

    def greet_all(self):
        barrier = pltpu.get_barrier_semaphore()
        me = self.dp * 4 + self.table
        for step in range(1, 32):
            other = (me + step) % 32
            pl.semaphore_signal(
                barrier, inc=1, device_id=(other // 4, other % 4), device_id_type=MESH
            )
        pl.semaphore_wait(barrier, 31)


class Spread:
    def __init__(self, net, shard, whole, split):
        self.net, self.shard, self.whole = net, shard, whole
        cols = shard.shape[1]
        self.first, self.second = pl.ds(0, split), pl.ds(split, cols - split)

    def start_line(self):
        net = self.net
        mine = self.whole.at[net.z, net.y, net.x, net.c]
        self.from_z = [None] + [
            net.send(self.shard, mine, net.at(z=net.line[step])) for step in (1, 2, 3)
        ]

    def start_sides(self):
        net = self.net
        mine = self.whole.at[net.z, net.y, net.x, net.c]
        self.from_x = [net.send(self.shard, mine, net.across_x())]
        self.from_y = [net.send(self.shard, mine, net.across_y())]

    def sides(self):
        net = self.net
        for step in (1, 2, 3):
            self.from_z[step].wait_recv()
            part = self.whole.at[net.line[step], net.y, net.x, net.c]
            self.from_x.append(net.send(part, part, net.across_x()))
            self.from_y.append(net.send(part, part, net.across_y()))

    def corners(self):
        net = self.net
        self.from_corner = []
        for step in range(4):
            self.from_x[step].wait_recv()
            part = self.whole.at[net.line[step], net.y, 1 - net.x, net.c, :, self.first]
            self.from_corner.append(net.send(part, part, net.across_y()))
            self.from_y[step].wait_recv()
            part = self.whole.at[net.line[step], 1 - net.y, net.x, net.c, :, self.second]
            self.from_corner.append(net.send(part, part, net.across_x()))

    def cores(self):
        net = self.net
        self.from_core = []
        self.kept.wait()
        for y, x in ((net.y, net.x), (net.y, 1 - net.x), (1 - net.y, net.x)):
            part = self.whole.at[:, y, x, net.c]
            self.from_core.append(net.send(part, part, net.across_c()))
        for copy in self.from_corner:
            copy.wait_recv()
        part = self.whole.at[:, 1 - net.y, 1 - net.x, net.c]
        self.from_core.append(net.send(part, part, net.across_c()))

    def finish(self):
        for copy in self.from_core:
            copy.wait_recv()


def ranks_of(mask, before, below):
    marks = mask.astype(LOW)
    within = dot(marks, before)
    rows = dot(marks, jnp.ones((128, 128), LOW))
    return within + dot(below, rows.astype(LOW))


def fetch_kernel(
    row_bits,
    capacity,
    ids_ref,
    expr_ref,
    table_ref,
    shard_one,
    shard_up,
    shard_down,
    hidden_ref,
    place_ref,
    asked_ref,
    whole_one,
    whole_up,
    whole_down,
    all_ids,
    grouped,
    rank_ref,
    rows_ref,
    place_dev,
    rows_table,
    chosen,
    found,
    partner,
    pair,
    owned,
    owned_far,
    picks,
    far,
    far_in,
    asked_cols,
    send_sems,
    recv_sems,
    local_sems,
):
    net = Net(send_sems, recv_sems)
    half = capacity // 2
    rows_dev, width = table_ref.shape
    table_copy = pltpu.make_async_copy(table_ref, rows_table, local_sems.at[0])
    table_copy.start()
    spreads = [
        Spread(net, shard_one, whole_one, 1664),
        Spread(net, shard_up, whole_up, 1536),
        Spread(net, shard_down, whole_down, 384),
    ]
    for index, spread in enumerate(spreads):
        copy = pltpu.make_async_copy(
            spread.shard, spread.whole.at[net.z, net.y, net.x, net.c], local_sems.at[1 + index]
        )
        copy.start()
        spread.kept = copy
    net.greet_all()
    me = net.dp * 4 + net.table
    all_ids[me] = ids_ref[...]
    ids_in = []
    for step in range(1, 32):
        other = (me + step) % 32
        ids_in.append(net.send(ids_ref, all_ids.at[me], (other // 4, other % 4)))
    spreads[0].start_line()
    spreads[0].start_sides()
    spreads[1].start_line()
    spreads[1].start_sides()
    spreads[2].start_sides()
    for copy in ids_in:
        copy.wait_recv()
    for group in range(8):
        for table in range(4):
            grouped[group, pl.ds(2 * table, 2), :] = all_ids[4 * group + table]

    lanes = lax.broadcasted_iota(jnp.int32, (128, 128), 1)
    subs = lax.broadcasted_iota(jnp.int32, (128, 128), 0)
    before = (subs < lanes).astype(LOW)
    low_sub = lax.broadcasted_iota(jnp.int32, (64, 64), 0)
    low_lane = lax.broadcasted_iota(jnp.int32, (64, 64), 1)
    below = ((low_lane < low_sub) & (low_lane // 8 == low_sub // 8)).astype(LOW)
    every = grouped[...].reshape(64, 128)
    owner = lax.shift_right_logical(every, row_bits)
    rows_ref[...] = jnp.bitwise_and(every, (1 << row_bits) - 1).astype(F32)
    mine = (owner == net.dp).astype(F32)
    rank_ref[...] = jnp.where(mine > 0, ranks_of(mine, before, below), -1.0)

    slot_sub = lax.broadcasted_iota(jnp.int32, (capacity, 128), 0).astype(F32)
    lane_row = lax.broadcasted_iota(jnp.int32, (capacity, 128), 1).astype(F32)

    def choose(step, base):
        group = (net.dp + step) % 8

        def gather_row(row, total):
            rank = rank_ref[pl.ds(group * 8 + row, 1), :]
            value = rows_ref[pl.ds(group * 8 + row, 1), :]
            return total + jnp.where(slot_sub == rank, value, 0.0)

        total = lax.fori_loop(0, 8, gather_row, jnp.zeros((capacity, 128), F32))
        column = jnp.broadcast_to(jnp.sum(total, axis=1, keepdims=True), (capacity, 128))
        spot = pl.ds(pl.multiple_of(group * half, 8), half)
        asked_cols[0, spot, :] = column[:half]
        asked_cols[1, spot, :] = column[half:]
        start = pl.multiple_of((step - base) * capacity, 8)

        def mark(block, carry):
            at = pl.multiple_of(block * 128, 128)
            hit = column == lane_row + (block * 128).astype(F32)
            chosen[pl.ds(start, capacity), pl.ds(at, 128)] = jnp.where(hit, 1.0, 0.0).astype(LOW)
            return carry

        lax.fori_loop(0, rows_dev // 128, mark, 0)

    def look_up(base):
        lax.fori_loop(base, base + 4, lambda step, carry: (choose(step, base), carry)[1], 0)

        def columns(block, carry):
            at = pl.multiple_of(block * 256, 256)
            value = dot(chosen[...], rows_table[:, pl.ds(at, 256)]).astype(LOW)
            found[pl.ds(base, 4), :, :, pl.ds(at, 256)] = value.reshape(4, 2, half, 256)
            return carry

        lax.fori_loop(0, width // 256, columns, 0)

    def add_pairs(base):
        for step in range(base, base + 4):
            mine_half = found[step, net.c].astype(F32)
            pair[pl.ds(step * half, half), :] = (mine_half + partner[step].astype(F32)).astype(LOW)

    table_copy.wait()
    look_up(0)
    pair_in = [net.send(found.at[pl.ds(0, 4), 1 - net.c], partner.at[pl.ds(0, 4)], net.across_c())]
    look_up(4)
    pair_in.append(
        net.send(found.at[pl.ds(4, 4), 1 - net.c], partner.at[pl.ds(4, 4)], net.across_c())
    )
    here = pl.ds(pl.multiple_of(net.dp * half, 8), half)
    rows_in = []
    for base in (0, 4):
        pair_in[base // 4].wait_recv()
        add_pairs(base)
        for step in range(base, base + 4):
            if step == 0:
                owned[here, :] = pair[pl.ds(0, half), :]
                continue
            other = (net.dp + step) % 8
            rows_in.append(
                net.send(pair.at[pl.ds(step * half, half), :], owned.at[here, :], (other, net.table))
            )
    spreads[2].start_line()
    spreads[0].sides()
    spreads[0].corners()
    for part in range(2):
        asked_ref[part] = jnp.transpose(asked_cols[part])[0:8, :]

    hits_owner = lax.shift_right_logical(grouped[net.dp], row_bits).astype(F32)
    owners = lax.broadcasted_iota(jnp.int32, (8, 8, 128), 0).astype(F32)
    hits = (hits_owner[None] == owners).astype(F32).reshape(64, 128)
    slot = jnp.sum((ranks_of(hits, before, below) * hits).reshape(8, 8, 128), axis=0)
    upper = (slot >= half).astype(F32)
    away = jnp.where(upper == net.c.astype(F32), 0.0, 8.0 * half)
    place = hits_owner * half + slot - upper * half + away
    place_ref[...] = place
    for table in range(4):
        place_dev[table] = place[2 * table : 2 * table + 2]
    wide_lane = lax.broadcasted_iota(jnp.int32, (128, 128), 1).astype(F32)

    def spread_marks(table, base):
        for row in range(2):
            line = place_dev[table, pl.ds(row, 1), :]
            column = jnp.transpose(jnp.broadcast_to(line, (128, 128)))

            def mark(block, carry):
                at = pl.multiple_of(block * 128, 128)
                hit = column == wide_lane + (block * 128).astype(F32)
                picks[pl.ds(base + 128 * row, 128), pl.ds(at, 128)] = jnp.where(hit, 1.0, 0.0).astype(LOW)
                return carry

            lax.fori_loop(0, 16 * half // 128, mark, 0)

    spread_marks(net.table, 0)
    spread_marks((1 - net.x) * 2 + net.c, 256)
    for copy in rows_in:
        copy.wait_recv()
    owned_in = net.send(owned, owned_far, net.across_c())
    owned_in.wait_recv()

    def select(base):
        marks = picks[pl.ds(base, 256), :]
        return dot(marks[:, : 8 * half], owned[...]) + dot(marks[:, 8 * half :], owned_far[...])

    far[...] = select(256).astype(LOW)
    far_copy = net.send(far, far_in, net.across_x())
    near = select(0) + expr_ref[...].astype(F32)
    spreads[1].sides()
    spreads[1].corners()
    spreads[0].cores()
    far_copy.wait_recv()
    hidden_ref[...] = near + far_in[...].astype(F32)
    spreads[2].sides()
    spreads[2].corners()
    spreads[1].cores()
    spreads[2].cores()
    for spread in spreads:
        spread.finish()
    net.close()


def fetch(ids, expr, table, shard_one, shard_up, shard_down, row_bits, capacity):
    tok, width = expr.shape
    half = capacity // 2
    rows_dev = table.shape[0]
    vmem = pl.BlockSpec(memory_space=pltpu.VMEM)
    hbm = pl.BlockSpec(memory_space=pl.ANY)

    def whole(shard):
        return jax.ShapeDtypeStruct((4, 2, 2, 2) + shard.shape, LOW)

    count = 31 + 3 * 23 + 2 + 7 + 2
    return pl.pallas_call(
        functools.partial(fetch_kernel, row_bits, capacity),
        out_shape=(
            jax.ShapeDtypeStruct((tok, width), F32),
            jax.ShapeDtypeStruct((8, 128), F32),
            jax.ShapeDtypeStruct((2, 8, 8 * half), F32),
            whole(shard_one),
            whole(shard_up),
            whole(shard_down),
        ),
        in_specs=[vmem, vmem, hbm, hbm, hbm, hbm],
        out_specs=(vmem, vmem, vmem, hbm, hbm, hbm),
        scratch_shapes=[
            pltpu.VMEM((32, 2, 128), jnp.int32),
            pltpu.VMEM((8, 8, 128), jnp.int32),
            pltpu.VMEM((64, 128), F32),
            pltpu.VMEM((64, 128), F32),
            pltpu.VMEM((4, 2, 128), F32),
            pltpu.VMEM((rows_dev, width), LOW),
            pltpu.VMEM((4 * capacity, rows_dev), LOW),
            pltpu.VMEM((8, 2, half, width), LOW),
            pltpu.VMEM((8, half, width), LOW),
            pltpu.VMEM((8 * half, width), LOW),
            pltpu.VMEM((8 * half, width), LOW),
            pltpu.VMEM((8 * half, width), LOW),
            pltpu.VMEM((2 * tok, 16 * half), LOW),
            pltpu.VMEM((tok, width), LOW),
            pltpu.VMEM((tok, width), LOW),
            pltpu.VMEM((2, 8 * half, 128), F32),
            pltpu.SemaphoreType.DMA((count,)),
            pltpu.SemaphoreType.DMA((count,)),
            pltpu.SemaphoreType.DMA((4,)),
        ],
        compiler_params=pltpu.CompilerParams(
            collective_id=0, has_side_effects=True, vmem_limit_bytes=60 * 2**20
        ),
        name="fetch",
    )(ids, expr, table, shard_one, shard_up, shard_down)


def dot_t(left, right):
    return lax.dot_general(left, right, (((1,), (1,)), ((), ())), preferred_element_type=F32)


def t_dot(left, right):
    return lax.dot_general(left, right, (((0,), (0,)), ((), ())), preferred_element_type=F32)


class Fold:
    def __init__(self, net, terms, mid, corner_y, corner_x, side_x, side_y, line, split):
        self.net, self.terms, self.mid = net, terms, mid
        self.corner_y, self.corner_x = corner_y, corner_x
        self.side_x, self.side_y, self.line = side_x, side_y, line
        cols = terms.shape[5]
        self.first, self.second = pl.ds(0, split), pl.ds(split, cols - split)

    def start(self):
        net = self.net
        self.core_in = net.send(self.terms.at[:, :, :, 1 - net.c], self.mid, net.across_c())

    def corners(self):
        net = self.net
        self.core_in.wait_recv()

        def add(z, carry):
            for y, x in ((1, 1), (0, 1), (1, 0), (0, 0)):
                self.mid[z, y, x] = (
                    self.mid[z, y, x].astype(F32) + self.terms[z, y, x, net.c].astype(F32)
                ).astype(LOW)
            return carry

        lax.fori_loop(0, 4, add, 0)
        self.corner_y_in = net.send(
            self.mid.at[:, 1 - net.y, 1 - net.x, :, self.first], self.corner_y, net.across_y()
        )
        self.corner_x_in = net.send(
            self.mid.at[:, 1 - net.y, 1 - net.x, :, self.second], self.corner_x, net.across_x()
        )

    def sides(self):
        net, mid = self.net, self.mid
        self.corner_y_in.wait_recv()

        def add_x(z, carry):
            mid[z, net.y, 1 - net.x, :, self.first] = (
                mid[z, net.y, 1 - net.x, :, self.first].astype(F32) + self.corner_y[z].astype(F32)
            ).astype(LOW)
            return carry

        lax.fori_loop(0, 4, add_x, 0)
        self.side_x_in = net.send(mid.at[:, net.y, 1 - net.x], self.side_x, net.across_x())
        self.corner_x_in.wait_recv()

        def add_y(z, carry):
            mid[z, 1 - net.y, net.x, :, self.second] = (
                mid[z, 1 - net.y, net.x, :, self.second].astype(F32) + self.corner_x[z].astype(F32)
            ).astype(LOW)
            return carry

        lax.fori_loop(0, 4, add_y, 0)
        self.side_y_in = net.send(mid.at[:, 1 - net.y, net.x], self.side_y, net.across_y())

    def lines(self):
        net, mid = self.net, self.mid
        self.side_x_in.wait_recv()
        self.side_y_in.wait_recv()

        def add(z, carry):
            mid[z, net.y, net.x] = (
                mid[z, net.y, net.x].astype(F32)
                + self.side_x[z].astype(F32)
                + self.side_y[z].astype(F32)
            ).astype(LOW)
            return carry

        lax.fori_loop(0, 4, add, 0)
        self.line_in = [
            net.send(
                mid.at[net.line[step], net.y, net.x],
                self.line.at[step - 1],
                net.at(z=net.line[step]),
            )
            for step in (1, 2, 3)
        ]

    def finish(self, out_ref):
        net = self.net
        for copy in self.line_in:
            copy.wait_recv()
        total = self.mid[net.z, net.y, net.x].astype(F32)
        for step in range(3):
            total = total + self.line[step].astype(F32)
        out_ref[...] = total


def centered(values):
    mean = jnp.mean(values, axis=-1, keepdims=True)
    center = values - mean
    spread = jnp.mean(center * center, axis=-1, keepdims=True)
    scale = lax.rsqrt(spread + 1e-05)
    return center * scale, scale


def centered_back(grad, unit, scale):
    mean = jnp.mean(grad, axis=-1, keepdims=True)
    along = jnp.mean(grad * unit, axis=-1, keepdims=True)
    return scale * (grad - mean - unit * along)


def col_sum(values):
    return jnp.sum(values, axis=0, keepdims=True)


BLOCK = 64


def layer_kernel(
    half,
    hidden_ref,
    cot_ref,
    lens_ref,
    place_ref,
    params_ref,
    up_ref,
    whole_one,
    whole_up,
    whole_down,
    out_ref,
    grad_ref,
    sum_one,
    sum_up,
    sum_down,
    arrived_own,
    arrived_far,
    w_one,
    w_up,
    w_down,
    hidden_low,
    projected,
    probs,
    mixed,
    unit_one,
    scale_one,
    normed_low,
    active,
    slope,
    grad_h2,
    grad_low,
    grad_project,
    small,
    up_sums,
    terms_one,
    terms_up,
    terms_down,
    mid_one,
    mid_up,
    mid_down,
    corner_y_one,
    corner_x_one,
    corner_y_up,
    corner_x_up,
    corner_y_down,
    corner_x_down,
    side_x_one,
    side_y_one,
    side_x_up,
    side_y_up,
    side_x_down,
    side_y_down,
    line_one,
    line_up,
    line_down,
    group_grads,
    choose,
    outgoing,
    send_sems,
    recv_sems,
    local_sems,
):
    net = Net(send_sems, recv_sems)
    tok, width = hidden_ref.shape
    ff = w_up.shape[1]
    loads = []
    for index, (source, target) in enumerate(
        ((whole_one, w_one), (whole_up, w_up), (whole_down, w_down))
    ):
        copy = pltpu.make_async_copy(source, target, local_sems.at[index])
        copy.start()
        loads.append(copy)
    barrier = pltpu.get_barrier_semaphore()
    for step in range(1, 8):
        pl.semaphore_signal(
            barrier, inc=1, device_id=((net.dp + step) % 8, net.table), device_id_type=MESH
        )
    pl.semaphore_signal(barrier, inc=1, device_id=net.across_x(), device_id_type=MESH)
    pl.semaphore_signal(barrier, inc=1, device_id=net.across_c(), device_id_type=MESH)
    pl.semaphore_wait(barrier, 9)
    fold_one = Fold(
        net, terms_one, mid_one, corner_y_one, corner_x_one, side_x_one, side_y_one, line_one, 1664
    )
    fold_up = Fold(
        net, terms_up, mid_up, corner_y_up, corner_x_up, side_x_up, side_y_up, line_up, 1536
    )
    fold_down = Fold(
        net, terms_down, mid_down, corner_y_down, corner_x_down, side_x_down, side_y_down, line_down, 384
    )

    def param(row):
        return params_ref[row : row + 1, :]

    lane = lax.broadcasted_iota(jnp.int32, (128, 128), 1).astype(F32)
    sub = lax.broadcasted_iota(jnp.int32, (128, 128), 0).astype(F32)
    left = lane < 64
    left_low = jnp.where(left, 1.0, 0.0).astype(LOW)
    right_low = jnp.where(left, 0.0, 1.0).astype(LOW)

    def rows_of(block):
        return pl.ds(pl.multiple_of(block * BLOCK, BLOCK), BLOCK)

    def keep_of(block):
        length = lens_ref[pl.ds(block // (tok // 2 // BLOCK), 1), :]
        place = (block % (tok // 2 // BLOCK)) * BLOCK
        return jnp.where(sub[:BLOCK] + place.astype(F32) < length, 1.0, 0.0)[:, :1]

    hidden_low[...] = hidden_ref[...].astype(LOW)
    loads[0].wait()

    def project(block, carry):
        at = pl.ds(pl.multiple_of(block * width, 128), width)
        shift = jnp.where(block == 0, param(2), jnp.where(block == 1, 0.0, param(3)))
        projected[:, at] = (dot(hidden_low[...], w_one[:, at]) + shift).astype(LOW)
        return carry

    lax.fori_loop(0, 3, project, 0)
    pairs = width // 128

    def head_at(step):
        rows = pl.ds(pl.multiple_of((step // pairs) * 128, 128), 128)
        start = (step % pairs) * 128
        return rows, [
            pl.ds(pl.multiple_of(start + width * part, 128), 128) for part in range(3)
        ]

    def attend(step, carry):
        rows, at = head_at(step)
        queries, keys, values = (projected[rows, place] for place in at)
        open_keys = lane < lens_ref[pl.ds(step // pairs, 1), :]
        parts = []
        for head, mask in enumerate((left_low, right_low)):
            scores = jnp.where(open_keys, dot_t(queries * mask, keys) * 0.125, -1e30)
            raised = jnp.exp(scores - jnp.max(scores, axis=-1, keepdims=True))
            prob = raised / jnp.sum(raised, axis=-1, keepdims=True)
            probs[2 * step + head] = prob
            parts.append(dot(prob.astype(LOW), values))
        mixed[rows, at[0]] = jnp.where(left, parts[0], parts[1]).astype(LOW)
        return carry

    lax.fori_loop(0, 2 * pairs, attend, 0)
    grad_ref[...] = dot(mixed[...], w_one[:, pl.ds(3 * width, width)])

    def first_norm(block, carry):
        rows = rows_of(block)
        unit, scale = centered(hidden_ref[rows, :] + grad_ref[rows, :] + param(4))
        unit_one[rows, :] = unit
        scale_one[rows, :] = jnp.broadcast_to(scale, (BLOCK, 128))
        normed_low[rows, :] = (unit * param(0) + param(6)).astype(LOW)
        return carry

    lax.fori_loop(0, tok // BLOCK, first_norm, 0)
    loads[1].wait()

    def expand(block, carry):
        at = pl.ds(pl.multiple_of(block * 512, 128), 512)
        inner = dot(normed_low[...], w_up[:, at]) + up_ref[:, at]
        bell = 0.5 * (1.0 + lax.erf(inner * 0.7071067811865476))
        active[:, at] = (inner * bell).astype(LOW)
        slope[:, at] = (
            bell + inner * jnp.exp(-0.5 * inner * inner) * 0.3989422804014327
        ).astype(slope.dtype)
        return carry

    lax.fori_loop(0, ff // 512, expand, 0)
    loads[2].wait()

    def contract(block, carry):
        at = pl.ds(pl.multiple_of(block * 256, 128), 256)
        grad_ref[:, at] = dot(active[...], w_down[:, at])
        return carry

    lax.fori_loop(0, width // 256, contract, 0)

    def second_norm(block, carry):
        rows = rows_of(block)
        normed = unit_one[rows, :] * param(0) + param(6)
        unit, scale = centered(normed + grad_ref[rows, :] + param(5))
        keep = keep_of(block)
        out_ref[rows, :] = ((unit * param(1) + param(7)) * keep).astype(LOW)
        grad = cot_ref[rows, :].astype(F32) * keep
        back = centered_back(grad * param(1), unit, scale)
        grad_h2[rows, :] = back
        back_low = back.astype(LOW)
        grad_low[rows, :] = back_low
        return (
            carry[0] + col_sum(grad * unit),
            carry[1] + col_sum(grad),
            carry[2] + col_sum(back_low.astype(F32)),
        )

    zero_row = jnp.zeros((1, width), F32)
    sums = lax.fori_loop(0, tok // BLOCK, second_norm, (zero_row, zero_row, zero_row))
    small[1:2, :], small[7:8, :], small[5:6, :] = sums

    def down_terms(block, carry):
        value = t_dot(active[:, pl.ds(pl.multiple_of(block * 768, 128), 768)], grad_low[...])
        terms_down[block] = value.reshape(terms_down.shape[1:]).astype(LOW)
        return carry

    lax.fori_loop(0, 4, down_terms, 0)
    fold_down.start()

    def inner_back(block, carry):
        at = pl.ds(pl.multiple_of(block * 512, 128), 512)
        value = dot_t(grad_low[...], w_down[at, :]) * slope[:, at].astype(F32)
        value_low = value.astype(LOW)
        active[:, at] = value_low
        up_sums[:, at] = jnp.broadcast_to(col_sum(value_low.astype(F32)), (8, 512))
        return carry

    lax.fori_loop(0, ff // 512, inner_back, 0)

    def up_terms(block, carry):
        at = pl.ds(pl.multiple_of(block * 512, 128), 512)
        value = t_dot(normed_low[...], active[:, at])
        terms_up[:, :, :, :, :, at] = value.reshape(terms_up.shape[:5] + (512,)).astype(LOW)
        return carry

    lax.fori_loop(0, ff // 512, up_terms, 0)
    fold_down.corners()
    fold_up.start()

    def normed_back(block, carry):
        at = pl.ds(pl.multiple_of(block * 256, 128), 256)
        grad_ref[:, at] = dot_t(active[...], w_up[at, :])
        return carry

    lax.fori_loop(0, width // 256, normed_back, 0)

    def first_back(block, carry):
        rows = rows_of(block)
        grad = grad_h2[rows, :] + grad_ref[rows, :]
        unit = unit_one[rows, :]
        back = centered_back(grad * param(0), unit, scale_one[rows, :][:, :1])
        grad_h2[rows, :] = back
        back_low = back.astype(LOW)
        grad_low[rows, :] = back_low
        return (
            carry[0] + col_sum(grad * unit),
            carry[1] + col_sum(grad),
            carry[2] + col_sum(back_low.astype(F32)),
        )

    sums = lax.fori_loop(0, tok // BLOCK, first_back, (zero_row, zero_row, zero_row))
    small[0:1, :], small[6:7, :], small[4:5, :] = sums
    fold_down.sides()
    fold_up.corners()
    value = t_dot(mixed[...], grad_low[...])
    terms_one[:, :, :, :, :, pl.ds(3 * width, width)] = value.reshape(
        terms_one.shape[:5] + (width,)
    ).astype(LOW)
    mixed[...] = dot_t(grad_low[...], w_one[:, pl.ds(3 * width, width)]).astype(LOW)

    def attend_back(step, carry):
        rows, at = head_at(step)
        queries, keys, values = (projected[rows, place] for place in at)
        grads = mixed[rows, at[0]]
        parts = []
        for head, mask in enumerate((left_low, right_low)):
            prob = probs[2 * step + head]
            grad_prob = dot_t(grads * mask, values)
            along = jnp.sum(prob * grad_prob, axis=-1, keepdims=True)
            grad_score = (prob * (grad_prob - along)).astype(LOW)
            parts.append(
                (
                    dot(grad_score, keys) * 0.125,
                    t_dot(grad_score, queries) * 0.125,
                    t_dot(prob.astype(LOW), grads),
                )
            )
        for part in range(3):
            grad_project[rows, at[part]] = jnp.where(left, parts[0][part], parts[1][part]).astype(LOW)
        return carry

    lax.fori_loop(0, 2 * pairs, attend_back, 0)
    fold_down.lines()
    fold_up.sides()

    def input_back(block, carry):
        at = pl.ds(pl.multiple_of(block * 256, 128), 256)
        grad_ref[:, at] = grad_h2[:, at] + dot_t(
            grad_project[...], w_one[at, pl.ds(0, 3 * width)]
        )
        return carry

    lax.fori_loop(0, width // 256, input_back, 0)
    group_grads[net.table] = grad_ref[...].astype(LOW)
    mine = group_grads.at[net.table]
    grads_x = net.send(mine, mine, net.across_x())
    grads_c = [net.send(mine, mine, net.across_c())]

    def project_terms(block, carry):
        at = pl.ds(pl.multiple_of(block * width, 128), width)
        value = t_dot(hidden_low[...], grad_project[:, at])
        terms_one[:, :, :, :, :, at] = value.reshape(terms_one.shape[:5] + (width,)).astype(LOW)
        return carry

    lax.fori_loop(0, 3, project_terms, 0)
    ones = jnp.ones((8, tok), LOW)
    small[2:3, :] = dot(ones, grad_project[:, pl.ds(0, width)])[0:1, :]
    small[3:4, :] = dot(ones, grad_project[:, pl.ds(2 * width, width)])[0:1, :]
    columns = jnp.transpose(jnp.concatenate([small[...], jnp.zeros((120, width), F32)], axis=0))
    columns = columns.reshape(32, width // 32, 128)
    spread = jnp.concatenate([up_sums[...], up_sums[...], jnp.zeros((112, ff), F32)], axis=0)
    spread = jnp.transpose(spread).reshape(32, ff // width, width // 32, 128)
    spot = lax.broadcasted_iota(jnp.int32, (32, width // 32, 128), 2)
    for part in range(ff // width):
        columns = jnp.where(spot == 8 + part, spread[:, part], columns)
    terms_one[:, :, :, :, :, pl.ds(4 * width, 128)] = columns.reshape(
        terms_one.shape[:5] + (128,)
    ).astype(LOW)
    fold_one.start()
    grads_x.wait_recv()
    part = group_grads.at[(1 - net.x) * 2 + net.c]
    grads_c.append(net.send(part, part, net.across_c()))

    def mark(block, carry):
        line = place_ref[pl.ds(block, 1), :]
        for piece in range(8 * half // 128):
            hit = sub + 128.0 * piece == line
            choose[pl.ds(128 * piece, 128), pl.ds(pl.multiple_of(block * 128, 128), 128)] = jnp.where(
                hit, 1.0, 0.0
            ).astype(LOW)
        return carry

    lax.fori_loop(0, 8, mark, 0)
    for copy in grads_c:
        copy.wait_recv()
    outgoing[...] = dot(choose[...], group_grads[...].reshape(4 * tok, width)).astype(LOW)
    here = pl.ds(pl.multiple_of(net.dp * half, 8), half)
    rows_in = []
    for step in range(8):
        other = (net.dp + step) % 8
        source = pl.ds(pl.multiple_of(other * half, 8), half)
        if step == 0:
            arrived_own[here, :] = outgoing[source, :]
        else:
            rows_in.append(
                net.send(outgoing.at[source, :], arrived_own.at[here, :], (other, net.table))
            )
    fold_up.lines()
    fold_one.corners()
    fold_down.finish(sum_down)
    for copy in rows_in:
        copy.wait_recv()
    rows_far = net.send(arrived_own, arrived_far, net.across_c())
    fold_one.sides()
    fold_up.finish(sum_up)
    fold_one.lines()
    fold_one.finish(sum_one)
    rows_far.wait_recv()
    net.close()


def layer(hidden, cot, lens, place, params, up_row, whole_one, whole_up, whole_down, half):
    tok, width = hidden.shape
    ff = whole_up.shape[1]
    wide = whole_one.shape[1]
    vmem = pl.BlockSpec(memory_space=pltpu.VMEM)
    hbm = pl.BlockSpec(memory_space=pl.ANY)
    rows = width // 32
    down_rows = ff // 32
    heads = width // HEAD_DIM

    def low(*shape):
        return pltpu.VMEM(shape, LOW)

    def full(*shape):
        return pltpu.VMEM(shape, F32)

    grid = (4, 2, 2)
    count = 3 * 8 + 4 + 7 + 1
    return pl.pallas_call(
        functools.partial(layer_kernel, half),
        out_shape=(
            jax.ShapeDtypeStruct((tok, width), LOW),
            jax.ShapeDtypeStruct((tok, width), F32),
            jax.ShapeDtypeStruct((rows, wide), F32),
            jax.ShapeDtypeStruct((rows, ff), F32),
            jax.ShapeDtypeStruct((down_rows, width), F32),
            jax.ShapeDtypeStruct((8 * half, width), LOW),
            jax.ShapeDtypeStruct((8 * half, width), LOW),
        ),
        in_specs=[vmem] * 6 + [hbm] * 3,
        out_specs=(vmem,) * 7,
        scratch_shapes=[
            low(width, wide),
            low(width, ff),
            low(ff, width),
            low(tok, width),
            low(tok, 3 * width),
            full(2 * heads, 128, 128),
            low(tok, width),
            full(tok, width),
            full(tok, 128),
            low(tok, width),
            low(tok, ff),
            low(tok, ff),
            full(tok, width),
            low(tok, width),
            low(tok, 3 * width),
            full(8, width),
            full(8, ff),
            low(*grid, 2, rows, wide),
            low(*grid, 2, rows, ff),
            low(*grid, 2, down_rows, width),
            low(*grid, rows, wide),
            low(*grid, rows, ff),
            low(*grid, down_rows, width),
            low(4, rows, 1664),
            low(4, rows, wide - 1664),
            low(4, rows, ff // 2),
            low(4, rows, ff // 2),
            low(4, down_rows, width // 2),
            low(4, down_rows, width // 2),
            low(4, rows, wide),
            low(4, rows, wide),
            low(4, rows, ff),
            low(4, rows, ff),
            low(4, down_rows, width),
            low(4, down_rows, width),
            low(3, rows, wide),
            low(3, rows, ff),
            low(3, down_rows, width),
            low(4, tok, width),
            low(8 * half, 4 * tok),
            low(8 * half, width),
            pltpu.SemaphoreType.DMA((count,)),
            pltpu.SemaphoreType.DMA((count,)),
            pltpu.SemaphoreType.DMA((3,)),
        ],
        compiler_params=pltpu.CompilerParams(
            collective_id=1, has_side_effects=True, vmem_limit_bytes=67043328
        ),
        name="layer",
    )(hidden, cot, lens, place, params, up_row, whole_one, whole_up, whole_down)


def place_kernel(asked_ref, own_ref, far_ref, out_ref):
    core = lax.axis_index("table") % 2
    rows, slots = out_ref.shape[0], own_ref.shape[0]
    base = (pl.program_id(0) * rows).astype(F32)
    row = lax.broadcasted_iota(jnp.int32, (rows, slots), 0).astype(F32) + base
    own = jnp.where(row == asked_ref[core, 0:1, :], 1.0, 0.0).astype(LOW)
    far = jnp.where(row == asked_ref[1 - core, 0:1, :], 1.0, 0.0).astype(LOW)
    out_ref[...] = dot(own, own_ref[...]) + dot(far, far_ref[...])


def place_rows(asked, own, far, rows_dev):
    slots, width = own.shape
    tile = 512 if rows_dev % 512 == 0 else 128
    return pl.pallas_call(
        place_kernel,
        grid=(rows_dev // tile,),
        out_shape=jax.ShapeDtypeStruct((rows_dev, width), F32),
        in_specs=[
            pl.BlockSpec(asked.shape, lambda step: (0, 0, 0)),
            pl.BlockSpec((slots, width), lambda step: (0, 0)),
            pl.BlockSpec((slots, width), lambda step: (0, 0)),
        ],
        out_specs=pl.BlockSpec((tile, width), lambda step: (step, 0)),
        name="place_rows",
    )(asked, own, far)


def layer_norm(values, scale, shift):
    center = values - jnp.mean(values, axis=-1, keepdims=True)
    spread = jnp.mean(center * center, axis=-1, keepdims=True)
    return center * lax.rsqrt(spread + 1e-05) * scale + shift


def gelu_exact(values):
    return jax.nn.gelu(values, approximate=False)


class Grid:
    def __init__(self):
        dp, table = lax.axis_size("dp"), lax.axis_size("table")
        self.count = dp * table
        self.high = dp // 2
        self.side = table // 2
        self.bit_core = 1
        self.bit_x = 2
        self.bit_y = table
        self.bit_z = 2 * table
        me_dp, me_table = lax.axis_index("dp"), lax.axis_index("table")
        self.z, self.y = me_dp // 2, me_dp % 2
        self.x, self.core = me_table // 2, me_table % 2

    def swap(self, value, mask):
        pairs = [(index, index ^ mask) for index in range(self.count)]
        return lax.ppermute(value, AXES, pairs)


def ordered(flag, own, other, axis):
    first = flag == 0
    return jnp.stack([jnp.where(first, own, other), jnp.where(first, other, own)], axis=axis)


def pick(values, index, axis):
    return lax.dynamic_index_in_dim(values, index, axis=axis, keepdims=False)


def gather_chunk(grid, shard, x_first):
    rows = [shard] + [grid.swap(shard, grid.bit_z * step) for step in range(1, grid.high)]
    line = jnp.stack(rows)
    place = jnp.arange(grid.high) ^ grid.z
    line = jnp.stack(
        [
            sum_select([(place[spot] == step, rows[step]) for step in range(grid.high)])
            for spot in range(grid.high)
        ]
    )
    first, second = (grid.bit_x, grid.bit_y) if x_first else (grid.bit_y, grid.bit_x)
    one = grid.swap(line, first)
    two = grid.swap(line, second)
    three = grid.swap(one, second)
    if x_first:
        own_y, other_y = ordered(grid.x, line, one, 1), ordered(grid.x, two, three, 1)
        plane = ordered(grid.y, own_y, other_y, 1)
    else:
        own_x, other_x = ordered(grid.y, line, one, 1), ordered(grid.y, two, three, 1)
        plane = ordered(grid.x, own_x, other_x, 2)
    partner = grid.swap(plane, grid.bit_core)
    whole = ordered(grid.core, plane, partner, 3)
    return whole.reshape((grid.count,) + shard.shape)


def sum_select(choices):
    result = choices[-1][1]
    for test, value in choices[:-1]:
        result = jnp.where(test, value, result)
    return result


def scatter_chunk(grid, grads, x_first):
    rows = grads.shape[0] // grid.count
    blocks = grads.reshape((grid.high, 2, grid.side, 2, rows, grads.shape[1]))
    low = jnp.bfloat16

    def halve(value, flag, axis, bit):
        sent = grid.swap(pick(value, 1 - flag, axis).astype(low), bit)
        return pick(value, flag, axis).astype(jnp.float32) + sent.astype(jnp.float32)

    part = halve(blocks, grid.core, 3, grid.bit_core).astype(low)
    if x_first:
        part = halve(part, grid.x, 2, grid.bit_x).astype(low)
        part = halve(part, grid.y, 1, grid.bit_y).astype(low)
    else:
        part = halve(part, grid.y, 1, grid.bit_y).astype(low)
        part = halve(part, grid.x, 1, grid.bit_x).astype(low)
    total = pick(part, grid.z, 0).astype(jnp.float32)
    for step in range(1, grid.high):
        total = total + grid.swap(pick(part, grid.z ^ step, 0), grid.bit_z * step).astype(jnp.float32)
    return total


def attend_scores(queries, key_rows, key_mask):
    scores = (
        jnp.einsum("sqhd,skhd->shqk", queries, key_rows, preferred_element_type=jnp.float32) * 0.125
    )
    return jnp.where(key_mask[:, None, None, :], scores, -1e30)


def layer_pass(weights, hidden_part, cot_part, length_part):
    w_qkv, w_out, w_up, w_down, gain_rows, shift_rows, up_shift = weights
    slots, seq, width = hidden_part.shape
    heads = width // HEAD_DIM
    count = slots * seq
    qkv_shift = jnp.concatenate([shift_rows[0], jnp.zeros_like(shift_rows[0]), shift_rows[1]])
    key_mask = jnp.arange(seq)[None, :] < length_part[:, None]
    row_keep = key_mask.reshape(count, 1).astype(jnp.float32)
    hidden_in = hidden_part.reshape(count, width)
    hidden_low = hidden_in.astype(jnp.bfloat16)
    projected = jnp.dot(hidden_low, w_qkv, preferred_element_type=jnp.float32) + qkv_shift
    project_low = projected.astype(jnp.bfloat16).reshape(slots, seq, 3, heads, HEAD_DIM)
    queries = project_low[:, :, 0]
    key_rows = project_low[:, :, 1]
    value_rows = project_low[:, :, 2]
    scores = attend_scores(queries, key_rows, key_mask)
    row_max = jnp.max(scores, axis=-1, keepdims=True)
    raised = jnp.exp(scores - row_max)
    row_total = jnp.sum(raised, axis=-1, keepdims=True)
    probs = raised / row_total
    probs_low = probs.astype(jnp.bfloat16)
    mixed = jnp.einsum("shqk,skhd->sqhd", probs_low, value_rows, preferred_element_type=jnp.float32)
    mixed_low = mixed.reshape(count, width).astype(jnp.bfloat16)
    branch = jnp.dot(mixed_low, w_out, preferred_element_type=jnp.float32) + shift_rows[2]
    normed, first_back = jax.vjp(layer_norm, hidden_in + branch, gain_rows[0], shift_rows[4])
    normed_low = normed.astype(jnp.bfloat16)
    inner = jnp.dot(normed_low, w_up, preferred_element_type=jnp.float32) + up_shift
    active, gelu_back = jax.vjp(gelu_exact, inner)
    active_low = active.astype(jnp.bfloat16)
    feed = jnp.dot(active_low, w_down, preferred_element_type=jnp.float32) + shift_rows[3]
    final, second_back = jax.vjp(layer_norm, normed + feed, gain_rows[1], shift_rows[5])
    output = (final * row_keep).astype(jnp.bfloat16).reshape(slots, seq, width)
    grad_final = cot_part.reshape(count, width).astype(jnp.float32) * row_keep
    grad_h2, grad_gain_two, grad_shift_two = second_back(grad_final)
    grad_feed = grad_h2.astype(jnp.bfloat16)
    grad_down = jnp.einsum("rf,rd->fd", active_low, grad_feed, preferred_element_type=jnp.float32)
    grad_down_shift = jnp.sum(grad_feed, axis=0, dtype=jnp.float32)
    grad_active = jnp.einsum("rd,fd->rf", grad_feed, w_down, preferred_element_type=jnp.float32)
    grad_inner = gelu_back(grad_active)[0].astype(jnp.bfloat16)
    grad_up = jnp.einsum("rd,rf->df", normed_low, grad_inner, preferred_element_type=jnp.float32)
    grad_up_shift = jnp.sum(grad_inner, axis=0, dtype=jnp.float32)
    grad_normed = grad_h2 + jnp.einsum(
        "rf,df->rd", grad_inner, w_up, preferred_element_type=jnp.float32
    )
    grad_h, grad_gain_one, grad_shift_one = first_back(grad_normed)
    grad_branch = grad_h.astype(jnp.bfloat16)
    grad_out = jnp.einsum("rd,re->de", mixed_low, grad_branch, preferred_element_type=jnp.float32)
    grad_out_shift = jnp.sum(grad_branch, axis=0, dtype=jnp.float32)
    grad_mixed = jnp.einsum("re,de->rd", grad_branch, w_out, preferred_element_type=jnp.float32)
    grad_mixed_low = grad_mixed.astype(jnp.bfloat16).reshape(slots, seq, heads, HEAD_DIM)
    grad_probs = jnp.einsum(
        "sqhd,skhd->shqk", grad_mixed_low, value_rows, preferred_element_type=jnp.float32
    )
    row_dot = jnp.sum(probs * grad_probs, axis=-1, keepdims=True)
    grad_scores = (probs * (grad_probs - row_dot)).astype(jnp.bfloat16)
    grad_queries = (
        jnp.einsum("shqk,skhd->sqhd", grad_scores, key_rows, preferred_element_type=jnp.float32)
        * 0.125
    )
    grad_keys = (
        jnp.einsum("shqk,sqhd->skhd", grad_scores, queries, preferred_element_type=jnp.float32)
        * 0.125
    )
    grad_values = jnp.einsum(
        "shqk,sqhd->skhd", probs_low, grad_mixed_low, preferred_element_type=jnp.float32
    )
    grad_project = jnp.concatenate(
        [
            grad_queries.reshape(count, width).astype(jnp.bfloat16),
            grad_keys.reshape(count, width).astype(jnp.bfloat16),
            grad_values.reshape(count, width).astype(jnp.bfloat16),
        ],
        axis=1,
    )
    grad_qkv = jnp.einsum("rd,re->de", hidden_low, grad_project, preferred_element_type=jnp.float32)
    project_sums = jnp.sum(grad_project, axis=0, dtype=jnp.float32)
    grad_input = grad_h + jnp.einsum(
        "re,de->rd", grad_project, w_qkv, preferred_element_type=jnp.float32
    )
    small = jnp.stack(
        [
            grad_gain_one,
            grad_gain_two,
            project_sums[:width],
            project_sums[2 * width :],
            grad_out_shift,
            grad_down_shift,
            grad_shift_one,
            grad_shift_two,
        ]
    )
    return (output, grad_input.reshape(slots, seq, width), grad_qkv, grad_out, grad_up, grad_down, small, grad_up_shift)


def one_hot(places, size):
    return (places[:, None] == jnp.arange(size, dtype=jnp.int32)[None, :]).astype(jnp.bfloat16)


def local(
    expr,
    gene_owner,
    gene_row,
    lengths,
    cotangent,
    tables,
    w_qkv,
    w_out,
    w_up,
    w_down,
    gains,
    biases,
    up_bias,
):
    grid = Grid()
    micro, seq, width = expr.shape
    tok = micro * seq
    n_dp, n_table = lax.axis_size("dp"), lax.axis_size("table")
    group = n_table * tok
    capacity = 6 * tok // n_dp
    half = capacity // 2
    rows_dev = tables.shape[1]
    me_dp = lax.axis_index("dp")
    me_table = lax.axis_index("table")
    low = jnp.bfloat16

    part_rows = w_qkv.shape[0]
    up_cols = up_bias.shape[0] // part_rows
    small_cols = 8 + up_cols
    small = jnp.concatenate(
        [gains.T, biases.T, up_bias.reshape(up_cols, part_rows).T], axis=1
    )
    small = jnp.pad(small, ((0, 0), (0, 128 - small_cols)))
    shard_one = jnp.concatenate([w_qkv, w_out, small], axis=1)

    fast = (n_dp, n_table, seq, micro, width) == (8, 4, 128, 2, 768) and rows_dev % 128 == 0
    if fast:
        row_bits = rows_dev.bit_length()
        ids = gene_owner.reshape(micro, seq) * (1 << row_bits) + gene_row
        hidden, place, asked, one, two, full_down = fetch(
            ids, expr.reshape(tok, width), tables[0], shard_one, w_up, w_down, row_bits, capacity
        )
        wide = 3 * width
        count = grid.count
        one = one.reshape(count * part_rows, -1)
        small_all = one[:, wide + width : wide + width + small_cols].astype(F32)
        up_row = small_all[:, 8:].reshape(count, part_rows, up_cols).transpose(0, 2, 1).reshape(1, -1)
        lens = jnp.broadcast_to(lengths.astype(F32)[:, None], (micro, 128))
        out, grad_expr, sum_one, sum_up, sum_down, own, far = layer(
            hidden,
            cotangent.reshape(tok, width),
            lens,
            place,
            small_all[:, :8].T,
            up_row,
            one,
            two.reshape(count * part_rows, -1),
            full_down.reshape(count * w_down.shape[0], -1),
            half,
        )
        table_grad = place_rows(asked, own, far, rows_dev)
        sum_small = sum_one[:, wide + width :]
        return (
            out.reshape(expr.shape),
            grad_expr.reshape(expr.shape),
            table_grad[None],
            sum_one[:, :wide],
            sum_one[:, wide : wide + width],
            sum_up,
            sum_down,
            sum_small[:, :2].T,
            sum_small[:, 2:8].T,
            sum_small[:, 8:small_cols].T.reshape(-1),
        )
    ids = gene_owner.reshape(tok) * rows_dev + gene_row.reshape(tok)
    all_ids = lax.all_gather(ids, AXES, axis=0, tiled=True).reshape(n_dp, group)
    all_owner = all_ids // rows_dev
    all_row = all_ids - all_owner * rows_dev
    mine = all_owner == me_dp
    ranks = jnp.cumsum(mine.astype(jnp.int32), axis=1) - 1
    match = mine[:, None, :] & (ranks[:, None, :] == jnp.arange(capacity, dtype=jnp.int32)[None, :, None])
    asked = jnp.sum(jnp.where(match, all_row[:, None, :], 0), axis=2)

    group_owner = pick(all_owner, me_dp, 0)
    hits = (group_owner[:, None] == jnp.arange(n_dp, dtype=jnp.int32)[None, :]).astype(jnp.int32)
    earlier = jnp.cumsum(hits, axis=0) - hits
    slot_index = jnp.sum(earlier * hits, axis=1)
    in_own = (slot_index // half) == grid.core
    place = jnp.where(in_own, 0, n_dp * half) + group_owner * half + slot_index % half
    place_dev = place.reshape(n_table, tok)

    found = jnp.take(tables[0], asked.reshape(-1), axis=0).reshape(n_dp, 2, half, width)
    sent = grid.swap(pick(found, 1 - grid.core, 1), grid.bit_core)
    pair = (pick(found, grid.core, 1).astype(jnp.float32) + sent.astype(jnp.float32)).astype(low)
    returned = lax.all_to_all(pair, "dp", split_axis=0, concat_axis=0, tiled=True)
    returned_other = grid.swap(returned, grid.bit_core)
    slots_all = jnp.concatenate(
        [returned.reshape(n_dp * half, width), returned_other.reshape(n_dp * half, width)]
    )
    own_place = pick(place_dev, me_table, 0)
    far_place = pick(place_dev, me_table ^ grid.bit_x, 0)
    far = jnp.dot(one_hot(far_place, 2 * n_dp * half), slots_all, preferred_element_type=jnp.float32)
    near = jnp.dot(one_hot(own_place, 2 * n_dp * half), slots_all, preferred_element_type=jnp.float32)
    embedded = near + grid.swap(far.astype(low), grid.bit_x).astype(jnp.float32)
    hidden = expr.astype(jnp.float32) + embedded.reshape(micro, seq, width)

    one = gather_chunk(grid, shard_one, True)
    two = gather_chunk(grid, w_up, False)
    full_down = gather_chunk(grid, w_down, True)
    return finish(grid, hidden, place_dev, asked, one, two, full_down, expr, tables, lengths, cotangent, w_qkv, w_down, up_cols)


def finish(grid, hidden, place_dev, asked, one, two, full_down, expr, tables, lengths, cotangent, w_qkv, w_down, up_cols):
    micro, seq, width = expr.shape
    tok = micro * seq
    n_dp, n_table = lax.axis_size("dp"), lax.axis_size("table")
    capacity = 6 * tok // n_dp
    half = capacity // 2
    rows_dev = tables.shape[1]
    me_table = lax.axis_index("table")
    low = jnp.bfloat16
    part_rows = w_qkv.shape[0]
    small_cols = 8 + up_cols
    one = one.reshape(grid.count * part_rows, -1)
    two = two.reshape(grid.count * part_rows, -1)
    full_down = full_down.reshape(grid.count * w_down.shape[0], -1)
    wide = w_qkv.shape[1]
    small_all = one[:, wide + width :].astype(jnp.float32)
    gain_rows = small_all[:, :2].T
    bias_rows = small_all[:, 2:8].T
    up_all = (
        small_all[:, 8:small_cols].reshape(grid.count, part_rows, up_cols).transpose(0, 2, 1).reshape(-1)
    )
    weights = (one[:, :wide], one[:, wide : wide + width], two, full_down, gain_rows, bias_rows, up_all)
    out, grad_expr, grad_qkv, grad_out, grad_up, grad_down, grad_small, grad_up_bias = layer_pass(
        weights, hidden, cotangent, lengths
    )

    sum_down = scatter_chunk(grid, grad_down, True)
    sum_up = scatter_chunk(grid, grad_up, False)
    small_cat = jnp.concatenate(
        [
            grad_small.T,
            grad_up_bias.reshape(grid.count, up_cols, part_rows).transpose(0, 2, 1).reshape(-1, up_cols),
        ],
        axis=1,
    )
    small_cat = jnp.pad(small_cat, ((0, 0), (0, 128 - small_cols)))
    sum_one = scatter_chunk(grid, jnp.concatenate([grad_qkv, grad_out, small_cat], axis=1), True)
    sum_small = sum_one[:, wide + width :]

    flat = grad_expr.reshape(tok, width).astype(low)
    flat_x = grid.swap(flat, grid.bit_x)
    flat_c = grid.swap(flat, grid.bit_core)
    flat_xc = grid.swap(flat_x, grid.bit_core)
    group_grads = jnp.concatenate([flat, flat_c, flat_x, flat_xc])
    places = jnp.concatenate([pick(place_dev, me_table ^ step, 0) for step in range(n_table)])
    choose = (jnp.arange(n_dp * half, dtype=jnp.int32)[:, None] == places[None, :]).astype(low)
    outgoing = jnp.dot(choose, group_grads, preferred_element_type=jnp.float32).astype(low)
    incoming = lax.all_to_all(
        outgoing.reshape(n_dp, half, width), "dp", split_axis=0, concat_axis=0, tiled=True
    )
    incoming_other = grid.swap(incoming, grid.bit_core)
    arrived = ordered(grid.core, incoming, incoming_other, 1).reshape(n_dp * capacity, width)
    table_grad = jax.ops.segment_sum(
        arrived.astype(jnp.float32), asked.reshape(-1), num_segments=rows_dev
    )
    return (
        out,
        grad_expr,
        table_grad[None],
        sum_one[:, :wide],
        sum_one[:, wide : wide + width],
        sum_up,
        sum_down,
        sum_small[:, :2].T,
        sum_small[:, 2:8].T,
        sum_small[:, 8:small_cols].T.reshape(-1),
    )


def solution(mesh):
    both = ("dp", "table")
    placed = (
        P(both, None, None),
        P(both, None, None),
        P(both, None),
        P(both),
        P(both, None, None),
        P("table", "dp", None),
        P(both, None),
        P(both, None),
        P(both, None),
        P(both, None),
        P(None, both),
        P(None, both),
        P(both),
    )
    return jax.shard_map(
        local,
        mesh=mesh,
        in_specs=placed,
        out_specs=(
            P(both, None, None),
            P(both, None, None),
            P("table", "dp", None),
            P(both, None),
            P(both, None),
            P(both, None),
            P(both, None),
            P(None, both),
            P(None, both),
            P(both),
        ),
        check_vma=False,
    )
```
